1024 devices in a mesh: seq: 64 (over y, z_hi, x), head: 16 (over z_lo, core).
Axes of the slice: x: 4, y: 4, z: 32 (z_hi: 4, z_lo: 8; z = z_hi * 8 + z_lo), core: 2. Of those that a mesh axis runs over, the one named last changes fastest.
Arguments:
- queries: bfloat16 [32768, 64, 128], P('seq', 'head'), may hold values from -48 to 48
- keys_values: bfloat16 [32768, 2, 8, 128], P('seq'), may hold values from -6 to 6
- grad_out: bfloat16 [32768, 64, 128], P('seq', 'head'), may hold values from -6 to 6
- segments: int32 [32768], P('seq'), may hold values from 0 to 14, as said below
- partner: int32 [64], replicated, may hold values from 0 to 63, as said below
- prompt_blocks: int32 [64], replicated, may hold values from 1 to 4, as said below
Outputs:
- attention: bfloat16 [32768, 64, 128], P('seq', 'head')
- query_gradient: bfloat16 [32768, 64, 128], P('seq', 'head')
- kv_grad: bfloat16 [32768, 2048], P('seq', 'head')
The draws below stay inside these ranges and needn't reach their ends.
Inputs may be any that keep to these rules, and one draw needn't show every extreme that they name: `segments`: within each bin ids never fall; segment 0 begins at the bin's first token and holds more than 64 tokens; segment 1 follows it directly and is the bin's rejected response; the largest id is reached in some bin in every draw. partner[b] != b, every bin is the partner of exactly one bin, and following partner from any bin visits all bins. `prompt_blocks`: the largest value is reached in every draw.
All inputs are finite; a program needn't handle non-finite values.
Results may differ from the reference program's by a relative error of at most 0.025.
Values may be sent and summed in bfloat16 or wider, within the bound.
No kernel may reach another device: no remote copies, remote signals or barrier semaphores. Data moves between devices by JAX's collectives and lax.ppermute only.
A program may use at most 32 MiB of HBM per device.

```python
import math
import jax
import jax.numpy as jnp
from jax import lax

HEADS = 64
KVH = 8
HD = 128
TOK_DEV = 512
PMAX = 64
BLK = 16
EXTRA_CUTS = 12
NBINS = 64
TOKENS = 32768
N_HEAD = 16


def paired_floats(key):
    query_key = jax.random.fold_in(key, 101)
    kv_key = jax.random.fold_in(key, 202)
    kv_values = jnp.clip(jax.random.normal(kv_key, (TOKENS, 2, KVH, HD), jnp.float32), -6.0, 6.0)
    query_values = jnp.clip(jax.random.normal(query_key, (TOKENS, HEADS, HD), jnp.float32), -6.0, 6.0)
    return (query_values, kv_values)


def draw_queries(key, part):
    query_values, kv_values = paired_floats(key)
    return query_values.astype(jnp.bfloat16)


def draw_keys_values(key, part):
    query_values, kv_values = paired_floats(key)
    return kv_values.astype(jnp.bfloat16)


def draw_segments(key, part):
    bin_keys = jax.random.split(jax.random.fold_in(key, 606), NBINS)
    full_spot = jax.random.randint(jax.random.fold_in(key, 616), (), 0, NBINS)
    full_flags = jnp.arange(NBINS) == full_spot

    def one_bin(bin_key, full_flag):
        first_key, second_key, start_key, dense_key, live_key = jax.random.split(bin_key, 5)
        first_cut = jax.random.randint(first_key, (), PMAX + 8, TOK_DEV // 2)
        second_cut = first_cut + jax.random.randint(second_key, (), 8, TOK_DEV // 4)
        starts = jax.random.randint(start_key, (EXTRA_CUTS,), 0, TOK_DEV)
        density = jnp.where(full_flag, 4, jax.random.randint(dense_key, (), 0, 4))
        live_cuts = jax.random.randint(live_key, (EXTRA_CUTS,), 0, 4) < density
        starts = jnp.where(live_cuts, jnp.maximum(starts, second_cut), TOK_DEV)
        cuts = jnp.concatenate([jnp.stack([first_cut, second_cut]), starts])
        places = jnp.arange(TOK_DEV)
        return jnp.sum((places[:, None] >= cuts[None, :]).astype(jnp.int32), axis=1)
    return jax.vmap(one_bin)(bin_keys, full_flags).reshape(TOKENS).astype(jnp.int32)


def draw_partner(key, part):
    ranks = jax.random.permutation(jax.random.fold_in(key, 707), NBINS).astype(jnp.int32)
    anchor = jax.random.randint(jax.random.fold_in(key, 717), (), 0, NBINS).astype(jnp.int32)
    half = NBINS // 2
    fixed = jnp.stack([anchor, anchor - 1, anchor - 1 + half, anchor + half]) % NBINS
    ranks = ranks.at[fixed].set(jnp.arange(4, dtype=jnp.int32) - 4)
    order = jnp.argsort(ranks, stable=True).astype(jnp.int32)
    following = jnp.roll(order, -1)
    return jnp.zeros((NBINS,), jnp.int32).at[order].set(following)


def draw_prompt_blocks(key, part):
    value_key = jax.random.fold_in(key, 808)
    spot_key = jax.random.fold_in(key, 909)
    values = jax.random.randint(value_key, (NBINS,), 1, PMAX // BLK + 1)
    spot = jax.random.randint(spot_key, (), 0, NBINS)
    return values.at[spot].set(PMAX // BLK).astype(jnp.int32)


def block_scale(own_key, dims, pieces, smallest, high):
    def one(dim, parts):
        draws = jax.random.uniform(jax.random.fold_in(jax.random.fold_in(own_key, 6), dim), (parts,), jnp.float32, smallest / len(pieces), high / len(pieces))
        return jnp.repeat(jnp.exp(draws), dims[dim] // parts).reshape((-1,) + (1,) * (len(dims) - dim - 1))

    level = one(*pieces[0])
    for cut in pieces[1:]:
        level = level * one(*cut)
    return level


def gaussian(key, shape, deviation, limit, cuts=(), kind=jnp.bfloat16):
    entries = deviation * jax.random.normal(key, shape, jnp.float32)
    if cuts:
        entries = entries * block_scale(key, shape, cuts, -0.22, 0.18)
    return jnp.clip(entries, -limit, limit).astype(kind)


def setup_inputs(seed: int = 0) -> dict:
    streams_of = jax.random.split(jax.random.key(seed), 7)
    return {
        "queries": draw_queries(jax.random.fold_in(streams_of[6], 71), 0),
        "keys_values": draw_keys_values(jax.random.fold_in(streams_of[6], 71), 0),
        "grad_out": gaussian(streams_of[2], (TOKENS, HEADS, HD), 1.0, 6.0, ((0, 64), (1, 16))),
        "segments": draw_segments(jax.random.fold_in(streams_of[6], 71), 0),
        "partner": draw_partner(jax.random.fold_in(streams_of[6], 71), 0),
        "prompt_blocks": draw_prompt_blocks(jax.random.fold_in(streams_of[6], 71), 0),
    }


def expanded_product(form, left, right):
    return jnp.einsum(form, left.astype(jnp.float32), right.astype(jnp.float32), precision=lax.Precision.HIGHEST)

def reference(queries, keys_values, grad_out, segments, partner, prompt_blocks):
    group_size = HEADS // KVH
    run_size = min(HEADS // N_HEAD, group_size)
    score_scaling = 1.0 / math.sqrt(HD)
    query_bins = queries.reshape(NBINS, TOK_DEV, KVH, group_size, HD)
    grad_bins = grad_out.reshape(NBINS, TOK_DEV, KVH, group_size, HD)
    kv_bins = keys_values.reshape(NBINS, TOK_DEV, 2, KVH, HD)
    seg_bins = segments.reshape(NBINS, TOK_DEV)
    prompt_bins = kv_bins[:, :PMAX]
    positions = jnp.arange(TOK_DEV, dtype=jnp.int32)
    prompt_places = jnp.arange(PMAX, dtype=jnp.int32)

    def run_sums(head_grads):
        rows_count = head_grads.shape[0]
        runs = head_grads.reshape(rows_count, KVH, group_size // run_size, run_size, HD)
        partial_sums = lax.optimization_barrier(jnp.sum(runs, axis=3)).astype(jnp.bfloat16)
        return lax.optimization_barrier(jnp.sum(partial_sums.astype(jnp.float32), axis=2))

    def one_bin(bin_index):
        owner_bin = partner[bin_index]
        query_tile = query_bins[bin_index]
        gradient_tile = grad_bins[bin_index]
        kv_block = kv_bins[bin_index]
        seg_block = seg_bins[bin_index]
        remote = prompt_bins[owner_bin]
        every_key_row = jnp.concatenate([kv_block[:, 0], remote[:, 0]], axis=0)
        every_value_row = jnp.concatenate([kv_block[:, 1], remote[:, 1]], axis=0)
        local_ok = (seg_block[:, None] == seg_block[None, :]) & (positions[None, :] <= positions[:, None])
        live_count = BLK * prompt_blocks[owner_bin]
        remote_ok = (seg_block[:, None] == 1) & (prompt_places[None, :] < live_count)
        allowed = jnp.concatenate([local_ok, remote_ok], axis=1)[None, None]
        score_matrix = expanded_product('imwh,lmh->mwil', query_tile, every_key_row) * score_scaling
        score_matrix = jnp.where(allowed, score_matrix, -jnp.inf)
        row_peak = lax.optimization_barrier(jnp.max(score_matrix, axis=-1, keepdims=True))
        weights_raw = jnp.where(allowed, jnp.exp(score_matrix - row_peak), jnp.float32(0.0))
        probabilities = weights_raw / lax.optimization_barrier(jnp.sum(weights_raw, axis=-1, keepdims=True))
        probability_lowprec = probabilities.astype(jnp.bfloat16)
        attention = expanded_product('aqiu,uax->iaqx', probability_lowprec, every_value_row).astype(jnp.bfloat16)
        row_delta = lax.optimization_barrier(jnp.sum(gradient_tile.astype(jnp.float32) * attention.astype(jnp.float32), axis=-1))
        row_delta = jnp.transpose(row_delta, (1, 2, 0))
        probability_gradient = expanded_product('imwh,lmh->mwil', gradient_tile, every_value_row)
        score_gradient = (probabilities * (probability_gradient - row_delta[..., None])).astype(jnp.bfloat16)
        query_gradient = (expanded_product('aqiu,uax->iaqx', score_gradient, every_key_row) * score_scaling).astype(jnp.bfloat16)
        key_head_rows = expanded_product('bjek,ebjz->kbjz', score_gradient, query_tile) * score_scaling
        value_head_rows = expanded_product('bjek,ebjz->kbjz', probability_lowprec, gradient_tile)
        stacked = jnp.stack([run_sums(key_head_rows), run_sums(value_head_rows)], axis=2)
        flat_grads = stacked.reshape(stacked.shape[0], 2 * KVH * HD)
        return (attention.reshape(TOK_DEV, HEADS, HD), query_gradient.reshape(TOK_DEV, HEADS, HD), flat_grads[:TOK_DEV], flat_grads[TOK_DEV:])
    attention, query_gradient, local_sums, remote_sums = lax.map(one_bin, jnp.arange(NBINS, dtype=jnp.int32))
    prompt_low = remote_sums.astype(jnp.bfloat16)
    source_of = jnp.zeros((NBINS,), jnp.int32).at[partner].set(jnp.arange(NBINS, dtype=jnp.int32))
    arrived = prompt_low[source_of].astype(jnp.float32)
    merged = local_sums.at[:, :PMAX].add(arrived)
    kv_grad = merged.astype(jnp.bfloat16).reshape(TOKENS, 2 * KVH * HD)
    return (attention.reshape(TOKENS, HEADS, HD), query_gradient.reshape(TOKENS, HEADS, HD), kv_grad)
```

```python
import math

import jax
import jax.numpy as jnp
from jax import lax
from jax.sharding import Mesh
from jax.sharding import PartitionSpec as P

HEADS = 64
KVH = 8
PMAX = 64
BLK = 16

NY, NW, NX, NH, NC = 4, 4, 4, 8, 2


def run_pairs(moves):
    pairs = []
    for w in range(NW):
        for sh, sc, shift, th, tc in moves:
            source = (w * NH + sh) * NC + sc
            target = ((w + shift) % NW * NH + th) * NC + tc
            pairs.append((source, target))
    return pairs


FORWARD_FAR = [(6 + d // 2, d % 2, 2, d, 0) for d in range(4)] + [
    (d // 2 - 2, d % 2, 2, d, 0) for d in range(4, 8)
]
FORWARD_NEXT = [(2 + d // 2, 1 - d % 2, 1, d, 1) for d in range(8)]
FORWARD_BACK = [(d // 2, d % 2, -1, d, 1) for d in range(8)]
BACKWARD_FAR = [(d, 0, 2, d, 0) for d in range(8)]
BACKWARD_NEXT = [(d, 1, 1, d, 1) for d in range(8)]
BACKWARD_BACK = [(d, 1, -1, d, 1) for d in range(8)]
RUN = ("w", "h", "c")
SWAP = [(0, 1), (1, 0)]


def head_table(moves):
    table = [0] * (NH * NC)
    for sh, sc, _, th, _ in moves:
        table[sh * NC + sc] = th
    return jnp.array(table, jnp.int32)


def coordinates(bin_index):
    return bin_index // (NW * NX), bin_index // NX % NW, bin_index % NX


def body(queries, keys_values, grad_out, segments, partner, prompt_blocks):
    rows_here = queries.shape[0]
    heads_here = queries.shape[1]
    head_dim = queries.shape[2]
    score_scaling = 1.0 / math.sqrt(head_dim)
    y, w, x = lax.axis_index("y"), lax.axis_index("w"), lax.axis_index("x")
    h, c = lax.axis_index("h"), lax.axis_index("c")
    self_index = (y * NW + w) * NX + x
    bin_ids = jnp.arange(NY * NW * NX, dtype=jnp.int32)
    inverse = jnp.sum(jnp.where(partner[None, :] == bin_ids[:, None], bin_ids[None, :], 0), axis=1)
    owner_bin = partner[self_index]
    yo, wo, xo = coordinates(owner_bin)

    prompts = keys_values[:PMAX]
    mine = h * NC + c

    def prompt_of(head):
        return lax.dynamic_index_in_dim(prompts, head, 2, keepdims=False)

    far_or_next = lax.ppermute(
        prompt_of(head_table(FORWARD_FAR + FORWARD_NEXT)[mine]), RUN,
        run_pairs(FORWARD_FAR + FORWARD_NEXT),
    )
    back = lax.ppermute(prompt_of(head_table(FORWARD_BACK)[mine]), RUN, run_pairs(FORWARD_BACK))
    own = prompt_of(h)
    first = jnp.where(c == 0, own, back)
    second = far_or_next
    slots = jnp.arange(NY * NX, dtype=jnp.int32)
    slot_bins = (slots // NX * NW + w) * NX + slots % NX
    slot_rel = (coordinates(partner[slot_bins])[1] - w) % NW
    take_first = slot_rel < 2
    outgoing = jnp.where(take_first[:, None, None, None], first[None], second[None])
    incoming = lax.all_to_all(outgoing, ("y", "x"), split_axis=0, concat_axis=0, tiled=True)
    got = lax.dynamic_index_in_dim(incoming, yo * NX + xo, 0, keepdims=False)
    other = lax.ppermute(got, "c", SWAP)
    remote = jnp.where((wo - w) % 2 == c, got, other)

    kv_local = lax.dynamic_index_in_dim(keys_values, h, 2, keepdims=False)
    every_key_row = jnp.concatenate([kv_local[:, 0], remote[:, 0]], axis=0)
    every_value_row = jnp.concatenate([kv_local[:, 1], remote[:, 1]], axis=0)

    positions = jnp.arange(rows_here, dtype=jnp.int32)
    local_ok = (segments[:, None] == segments[None, :]) & (positions[None, :] <= positions[:, None])
    live_count = BLK * prompt_blocks[owner_bin]
    remote_ok = (segments[:, None] == 1) & (jnp.arange(PMAX, dtype=jnp.int32)[None, :] < live_count)
    allowed = jnp.concatenate([local_ok, remote_ok], axis=1)[None]
    score_matrix = (
        jnp.einsum("iwh,lh->wil", queries, every_key_row, preferred_element_type=jnp.float32)
        * score_scaling
    )
    score_matrix = jnp.where(allowed, score_matrix, -jnp.inf)
    row_peak = jnp.max(score_matrix, axis=-1, keepdims=True)
    weights_raw = jnp.where(allowed, jnp.exp(score_matrix - row_peak), jnp.float32(0.0))
    probabilities = weights_raw / jnp.sum(weights_raw, axis=-1, keepdims=True)
    probability_lowprec = probabilities.astype(jnp.bfloat16)
    attention = jnp.einsum(
        "qiu,ux->iqx", probability_lowprec, every_value_row, preferred_element_type=jnp.float32
    ).astype(jnp.bfloat16)
    row_delta = jnp.sum(grad_out.astype(jnp.float32) * attention.astype(jnp.float32), axis=-1)
    row_delta = jnp.transpose(row_delta, (1, 0))
    probability_gradient = jnp.einsum(
        "iwh,lh->wil", grad_out, every_value_row, preferred_element_type=jnp.float32
    )
    score_gradient = (probabilities * (probability_gradient - row_delta[..., None])).astype(
        jnp.bfloat16
    )
    query_gradient = (
        jnp.einsum("qiu,ux->iqx", score_gradient, every_key_row, preferred_element_type=jnp.float32)
        * score_scaling
    ).astype(jnp.bfloat16)
    key_grad = (
        jnp.einsum("mox,omn->xn", score_gradient, queries, preferred_element_type=jnp.float32)
        * score_scaling
    )
    value_grad = jnp.einsum(
        "mox,omn->xn", probability_lowprec, grad_out, preferred_element_type=jnp.float32
    )
    kv_grads = jnp.stack([key_grad, value_grad], axis=0).astype(jnp.bfloat16)
    local_part = kv_grads[:, :rows_here]
    remote_part = kv_grads[:, rows_here:]

    remote_total = (
        remote_part.astype(jnp.float32) + lax.ppermute(remote_part, "c", SWAP).astype(jnp.float32)
    ).astype(jnp.bfloat16)
    spread = lax.all_to_all(
        jnp.broadcast_to(remote_total[None], (NY * NX, *remote_total.shape)),
        ("y", "x"), split_axis=0, concat_axis=0, tiled=True,
    )

    def parcel_for(shift):
        target = (y * NW + (w + shift) % NW) * NX + x
        yr, _, xr = coordinates(inverse[target])
        return lax.dynamic_index_in_dim(spread, yr * NX + xr, 0, keepdims=False)

    far_or_next_back = lax.ppermute(
        parcel_for(jnp.where(c == 0, 2, 1)), RUN, run_pairs(BACKWARD_FAR + BACKWARD_NEXT)
    )
    back_back = lax.ppermute(parcel_for(-1), RUN, run_pairs(BACKWARD_BACK))
    stay = parcel_for(0)
    rel = (coordinates(inverse[self_index])[1] - w) % NW
    arrived = jnp.where(c == 0, stay, back_back)
    arrived = jnp.where(rel < 2, arrived, far_or_next_back)
    arrived = jnp.where(rel % 2 == c, arrived, jnp.zeros((), arrived.dtype))
    kept = lax.dynamic_index_in_dim(local_part, c, 0, keepdims=False)
    given = lax.dynamic_index_in_dim(local_part, 1 - c, 0, keepdims=False)
    kept_prompt = lax.dynamic_index_in_dim(arrived, c, 0, keepdims=False)
    given_prompt = lax.dynamic_index_in_dim(arrived, 1 - c, 0, keepdims=False)
    swapped = lax.ppermute(given, "c", SWAP)
    swapped_prompt = lax.ppermute(given_prompt, "c", SWAP)
    own_sum = kept.astype(jnp.float32) + swapped.astype(jnp.float32)
    prompt_rows = (
        own_sum[:PMAX] + kept_prompt.astype(jnp.float32) + swapped_prompt.astype(jnp.float32)
    )
    kv_result = jnp.concatenate([prompt_rows, own_sum[PMAX:]], axis=0).astype(jnp.bfloat16)
    return (attention, query_gradient, kv_result)


def solution(mesh):
    fine = Mesh(mesh.devices.reshape(NY, NW, NX, NH, NC), ("y", "w", "x", "h", "c"))
    seq, head = ("y", "w", "x"), ("h", "c")
    in_specs = (
        P(seq, head, None),
        P(seq, None, None, None),
        P(seq, head, None),
        P(seq),
        P(),
        P(),
    )
    out_specs = (P(seq, head, None), P(seq, head, None), P(seq, head))
    return jax.shard_map(body, mesh=fine, in_specs=in_specs, out_specs=out_specs, check_vma=False)
```

```python
import math

import jax
import jax.numpy as jnp
from jax import lax
from jax.experimental import pallas as pl
from jax.experimental.pallas import tpu as pltpu
from jax.sharding import Mesh
from jax.sharding import PartitionSpec as P

HEADS = 64
KVH = 8
PMAX = 64
BLK = 16

NY, NW, NX, NH, NC = 4, 4, 4, 8, 2


def run_pairs(moves):
    pairs = []
    for w in range(NW):
        for sh, sc, shift, th, tc in moves:
            source = (w * NH + sh) * NC + sc
            target = ((w + shift) % NW * NH + th) * NC + tc
            pairs.append((source, target))
    return pairs


FORWARD_FAR = [(6 + d // 2, d % 2, 2, d, 0) for d in range(4)] + [
    (d // 2 - 2, d % 2, 2, d, 0) for d in range(4, 8)
]
FORWARD_NEXT = [(2 + d // 2, 1 - d % 2, 1, d, 1) for d in range(8)]
FORWARD_BACK = [(d // 2, d % 2, -1, d, 1) for d in range(8)]
BACKWARD_FAR = [(d, 0, 2, d, 0) for d in range(8)]
BACKWARD_NEXT = [(d, 1, 1, d, 1) for d in range(8)]
BACKWARD_BACK = [(d, 1, -1, d, 1) for d in range(8)]
RUN = ("w", "h", "c")
SWAP = [(0, 1), (1, 0)]


SCALE = 1.0 / math.sqrt(128)
LOG_SCALE = SCALE * math.log2(math.e)
MASKED = -1e30
QROWS = 512
PROWS = 256
TILE = 128


LOW, HIGH, LIVE, DIRECT, CORE, SLOT, FIRST, SEND_FAR, SEND_BACK, SEND_STAY, ARRIVAL = range(11)


def route(partner_ref, blocks_ref, segments_ref, table_ref):
    y, w, x = lax.axis_index("y"), lax.axis_index("w"), lax.axis_index("x")
    c = lax.axis_index("c")
    here = y * 16 + w * 4 + x
    owner = partner_ref[here]
    owner_w = (owner >> 2) & 3

    def seek(index, carry):
        far, back, stay, responder = carry
        mark = partner_ref[index]
        shift = (((mark >> 2) & 3) - w) & 3
        in_column = ((mark >> 4) == y) & ((mark & 3) == x)
        slot = ((index >> 4) << 2) | (index & 3)
        far = jnp.where(in_column & (shift == jnp.where(c == 0, 2, 1)), slot, far)
        back = jnp.where(in_column & (shift == 3), slot, back)
        stay = jnp.where(in_column & (shift == 0), slot, stay)
        return far, back, stay, jnp.where(mark == here, index, responder)

    zero = jnp.int32(0)
    far, back, stay, responder = lax.fori_loop(
        0, NY * NW * NX, seek, (zero, zero, zero, zero), unroll=8
    )
    first = zero
    for slot in range(NY * NX):
        wanted = partner_ref[(slot // NX) * 16 + w * 4 + slot % NX]
        first = first | jnp.where((((wanted >> 2) & 3) - w) & 3 < 2, 1 << slot, 0)
    segments = segments_ref[...]
    first_token = jnp.sum((segments < 1).astype(jnp.float32)).astype(jnp.int32)
    end_token = jnp.sum((segments < 2).astype(jnp.float32)).astype(jnp.int32)
    rel = (((responder >> 2) & 3) - w) & 3
    table_ref[LOW] = first_token >> 6
    table_ref[HIGH] = (end_token + 63) >> 6
    table_ref[LIVE] = BLK * blocks_ref[owner]
    table_ref[DIRECT] = (((owner_w - w) & 1) == c).astype(jnp.int32)
    table_ref[CORE] = c
    table_ref[SLOT] = ((owner >> 4) << 2) | (owner & 3)
    table_ref[FIRST] = first
    table_ref[SEND_FAR] = far
    table_ref[SEND_BACK] = back
    table_ref[SEND_STAY] = stay
    table_ref[ARRIVAL] = jnp.where((rel & 1) == c, jnp.where(rel < 2, 1, 2), 0)


def dot(left, right, left_dim, right_dim):
    return lax.dot_general(
        left, right, (((left_dim,), (right_dim,)), ((), ())), preferred_element_type=jnp.float32
    )


def local_scores(q, gate, keys, key_segments, step):
    width = TILE * (step + 1)
    scores = dot(q, keys[:width], 1, 1) + dot(gate, key_segments[:width], 1, 1)
    shape = (QROWS, TILE)
    token = lax.broadcasted_iota(jnp.int32, shape, 0) // 4
    causal = lax.broadcasted_iota(jnp.int32, shape, 1) <= token
    last = jnp.where(causal, scores[:, width - TILE :], MASKED)
    if step == 0:
        return last
    return jnp.concatenate([scores[:, : width - TILE], last], axis=1)


def local_forward(q_ref, gate_ref, kv_ref, keyseg_ref, out_ref, lse_ref):
    for step in range(4):
        rows = pl.ds(step * QROWS, QROWS)
        width = TILE * (step + 1)
        scores = local_scores(q_ref[rows, :], gate_ref[rows, :], kv_ref[0], keyseg_ref[...], step)
        peak = jnp.max(scores, axis=1, keepdims=True)
        weights = jnp.exp2((scores - peak) * LOG_SCALE)
        total = jnp.sum(weights, axis=1, keepdims=True)
        mixed = dot(weights.astype(jnp.bfloat16), kv_ref[1, :width, :], 1, 0)
        out_ref[rows, :] = mixed / total
        lse_ref[rows, :] = jnp.broadcast_to(peak * LOG_SCALE + jnp.log2(total), (QROWS, TILE))


def pick(scalars_ref, got_ref, other_ref):
    return jnp.where(scalars_ref[DIRECT] == 1, got_ref[...], other_ref[...])


def prompt_step(
    scalars_ref, q_ref, grad_ref, gate_ref, got_ref, other_ref, outin_ref, lsein_ref,
    out_ref, lse_ref, dscore_ref, dprompt_ref, dkey_ref, dvalue_ref,
):
    index = pl.program_id(0)

    @pl.when(index == 0)
    def _():
        dkey_ref[...] = jnp.zeros_like(dkey_ref)
        dvalue_ref[...] = jnp.zeros_like(dvalue_ref)

    @pl.when((scalars_ref[LOW] <= index) & (index < scalars_ref[HIGH]))
    def _():
        prompt = pick(scalars_ref, got_ref, other_ref)
        keys, values = prompt[:PMAX], prompt[PMAX:]
        segment_one = (lax.broadcasted_iota(jnp.int32, (PMAX, TILE), 1) == 1).astype(jnp.bfloat16)
        alive = lax.broadcasted_iota(jnp.int32, (PROWS, PMAX), 1) < scalars_ref[LIVE]
        q, grad = q_ref[...], grad_ref[...]
        scores = dot(q, keys, 1, 1) + dot(gate_ref[...], segment_one, 1, 1)
        logits = jnp.where(alive, scores, MASKED) * LOG_SCALE
        lse = lsein_ref[:, :1]
        peak = jnp.maximum(lse, jnp.max(logits, axis=1, keepdims=True))
        weights = jnp.exp2(logits - peak)
        before = jnp.exp2(lse - peak)
        total = before + jnp.sum(weights, axis=1, keepdims=True)
        inverse = 1.0 / total
        probabilities = weights * inverse
        low = probabilities.astype(jnp.bfloat16)
        out = outin_ref[...] * (before * inverse) + dot(low, values, 1, 0)
        out_ref[...] = out
        lse_ref[...] = jnp.broadcast_to(peak + jnp.log2(total), (PROWS, TILE))
        rounded = out.astype(jnp.bfloat16).astype(jnp.float32)
        delta = jnp.sum(grad.astype(jnp.float32) * rounded, axis=1, keepdims=True)
        dscore = (probabilities * (dot(grad, values, 1, 1) - delta)).astype(jnp.bfloat16)
        dscore_ref[...] = dscore
        dvalue_ref[...] += dot(low, grad, 0, 0)
        dkey_ref[...] += dot(dscore, q, 0, 0)

    @pl.when(index == pl.num_programs(0) - 1)
    def _():
        dprompt_ref[:PMAX, :] = (dkey_ref[...] * SCALE).astype(jnp.bfloat16)
        dprompt_ref[PMAX:, :] = dvalue_ref[...].astype(jnp.bfloat16)


def local_backward(
    scalars_ref, q_ref, grad_ref, gate_ref, kv_ref, keyseg_ref, got_ref, other_ref,
    outlocal_ref, lselocal_ref, outprompt_ref, lseprompt_ref, dscore_ref,
    attention_ref, dquery_ref, kept_ref, given_ref, dkey_ref, dvalue_ref, acc_ref,
):
    def chosen(prompt_ref, local_ref, step):
        parts = []
        for part in range(QROWS // PROWS):
            index = step * (QROWS // PROWS) + part
            inside = (scalars_ref[LOW] <= index) & (index < scalars_ref[HIGH])
            rows = pl.ds(index * PROWS, PROWS)
            parts.append(jnp.where(inside, prompt_ref[rows, :], local_ref[rows, :]))
        return jnp.concatenate(parts, axis=0)

    dkey_ref[...] = jnp.zeros_like(dkey_ref)
    dvalue_ref[...] = jnp.zeros_like(dvalue_ref)
    prompt_keys = pick(scalars_ref, got_ref, other_ref)[:PMAX]
    for step in range(4):
        rows = pl.ds(step * QROWS, QROWS)
        width = TILE * (step + 1)
        q, grad = q_ref[rows, :], grad_ref[rows, :]
        attention = chosen(outprompt_ref, outlocal_ref, step).astype(jnp.bfloat16)
        attention_ref[rows, :] = attention
        delta = jnp.sum(
            grad.astype(jnp.float32) * attention.astype(jnp.float32), axis=1, keepdims=True
        )
        scores = local_scores(q, gate_ref[rows, :], kv_ref[0], keyseg_ref[...], step)
        lse = chosen(lseprompt_ref, lselocal_ref, step)
        if step:
            lse = jnp.concatenate([lse] * (step + 1), axis=1)
        probabilities = jnp.exp2(scores * LOG_SCALE - lse)
        low = probabilities.astype(jnp.bfloat16)
        dprob = dot(grad, kv_ref[1, :width, :], 1, 1)
        dscore = (probabilities * (dprob - delta)).astype(jnp.bfloat16)
        acc_ref[...] = dot(dscore, kv_ref[0, :width, :], 1, 0)
        dvalue_ref[:width, :] += dot(low, grad, 0, 0)
        dkey_ref[:width, :] += dot(dscore, q, 0, 0)
        for part in range(QROWS // PROWS):
            index = step * (QROWS // PROWS) + part

            @pl.when((scalars_ref[LOW] <= index) & (index < scalars_ref[HIGH]))
            def _():
                acc_ref[pl.ds(part * PROWS, PROWS), :] += dot(
                    dscore_ref[pl.ds(index * PROWS, PROWS), :], prompt_keys, 1, 0
                )

        dquery_ref[rows, :] = (acc_ref[...] * SCALE).astype(jnp.bfloat16)
    dkey = dkey_ref[...] * SCALE
    dvalue = dvalue_ref[...]
    keep_key = scalars_ref[CORE] == 0
    kept_ref[...] = jnp.where(keep_key, dkey, dvalue).astype(jnp.bfloat16)
    given_ref[...] = jnp.where(keep_key, dvalue, dkey).astype(jnp.bfloat16)


SMEM = pl.BlockSpec(memory_space=pltpu.SMEM)
VMEM = pl.BlockSpec(memory_space=pltpu.VMEM)


def body(queries, keys_values, grad_out, segments, partner, prompt_blocks):
    rows_here = queries.shape[0]
    heads_here = queries.shape[1]
    head_dim = queries.shape[2]
    flat = rows_here * heads_here
    y, w, x = lax.axis_index("y"), lax.axis_index("w"), lax.axis_index("x")
    h, c = lax.axis_index("h"), lax.axis_index("c")

    zero = jnp.uint32(0)

    def prompt_of(head):
        rows = lax.dynamic_slice(
            keys_values, (zero, zero, head.astype(jnp.uint32), zero), (PMAX, 2, 1, head_dim)
        )
        return jnp.transpose(rows[:, :, 0], (1, 0, 2)).reshape(2 * PMAX, head_dim)

    far_sender = (h < 2) | (h >= 6)
    head_far = jnp.where(h < 2, 2 * h + c + 4, 2 * h + c - 12)
    head_next = 2 * h + 1 - c - 4
    far_or_next = lax.ppermute(
        prompt_of(jnp.where(far_sender, head_far, head_next)), RUN,
        run_pairs(FORWARD_FAR + FORWARD_NEXT),
    )
    back = lax.ppermute(
        prompt_of((2 * h + c) & (NH - 1)), RUN, run_pairs(FORWARD_BACK)
    )
    own = prompt_of(h)

    table = pl.pallas_call(
        route, out_shape=jax.ShapeDtypeStruct((16,), jnp.int32), name="route",
        in_specs=[SMEM, SMEM, VMEM], out_specs=SMEM,
    )(partner, prompt_blocks, segments.reshape(-1, TILE))

    kv_local = jnp.transpose(
        lax.dynamic_index_in_dim(keys_values, h.astype(jnp.uint32), 2, keepdims=False), (1, 0, 2)
    )
    lanes = jnp.arange(TILE, dtype=jnp.int32)
    row_segments = jnp.broadcast_to(segments[:, None], (rows_here, heads_here)).reshape(flat)
    gate = jnp.where(row_segments[:, None] == lanes[None, :], 0.0, MASKED).astype(jnp.bfloat16)
    key_segments = (segments[:, None] == lanes[None, :]).astype(jnp.bfloat16)
    q = queries.reshape(flat, head_dim)
    grad = grad_out.reshape(flat, head_dim)

    wide = jax.ShapeDtypeStruct((flat, head_dim), jnp.float32)
    narrow = jax.ShapeDtypeStruct((flat, head_dim), jnp.bfloat16)
    prompt_shape = jax.ShapeDtypeStruct((2 * PMAX, head_dim), jnp.bfloat16)
    part_shape = jax.ShapeDtypeStruct((rows_here, head_dim), jnp.bfloat16)
    local_out, local_lse = pl.pallas_call(
        local_forward, out_shape=(wide, wide), name="local_forward",
        in_specs=[VMEM] * 4, out_specs=(VMEM, VMEM),
    )(q, gate, kv_local, key_segments)
    scalar = [table[k].astype(jnp.uint32) for k in range(11)]

    slots = jnp.arange(NY * NX, dtype=jnp.uint32)
    first = jnp.where(c == 0, own, back)
    take_first = (scalar[FIRST] >> slots) & 1 == 1
    outgoing = jnp.where(take_first[:, None, None], first[None], far_or_next[None])
    outgoing, local_out, local_lse, scalar = lax.optimization_barrier(
        (outgoing, local_out, local_lse, scalar)
    )
    incoming = lax.all_to_all(outgoing, ("y", "x"), split_axis=0, concat_axis=0, tiled=True)
    got = lax.dynamic_index_in_dim(incoming, scalar[SLOT], 0, keepdims=False)
    other = lax.ppermute(got, "c", SWAP)

    def rows_block(index, table_ref):
        return jnp.clip(index, table_ref[LOW], table_ref[HIGH] - 1), 0

    def whole(index, table_ref):
        return 0, 0

    wide_block = pl.BlockSpec((PROWS, head_dim), rows_block)
    whole_block = pl.BlockSpec((2 * PMAX, head_dim), whole)
    out, lse, dscore, dprompt = pl.pallas_call(
        prompt_step,
        out_shape=(
            wide, wide, jax.ShapeDtypeStruct((flat, PMAX), jnp.bfloat16), prompt_shape,
        ),
        grid_spec=pltpu.PrefetchScalarGridSpec(
            num_scalar_prefetch=1,
            grid=(flat // PROWS,),
            in_specs=[wide_block] * 3 + [whole_block] * 2 + [wide_block] * 2,
            out_specs=(
                wide_block, wide_block, pl.BlockSpec((PROWS, PMAX), rows_block), whole_block,
            ),
            scratch_shapes=[pltpu.VMEM((PMAX, head_dim), jnp.float32)] * 2,
        ),
        name="prompt_step",
    )(table, q, grad, gate, got, other, local_out, local_lse)

    total = dprompt.astype(jnp.float32) + lax.ppermute(dprompt, "c", SWAP).astype(jnp.float32)
    spread = jnp.where(
        (slots == scalar[SLOT])[:, None, None], total.astype(jnp.bfloat16)[None],
        jnp.zeros((), jnp.bfloat16),
    )
    spread = lax.all_to_all(spread, ("y", "x"), split_axis=0, concat_axis=0, tiled=True)

    def parcel(slot):
        return lax.dynamic_index_in_dim(spread, slot, 0, keepdims=False)

    far_or_next_back = lax.ppermute(
        parcel(scalar[SEND_FAR]), RUN, run_pairs(BACKWARD_FAR + BACKWARD_NEXT)
    )
    back_back = lax.ppermute(parcel(scalar[SEND_BACK]), RUN, run_pairs(BACKWARD_BACK))
    stay = parcel(scalar[SEND_STAY])

    attention, query_gradient, kept, given = pl.pallas_call(
        local_backward,
        out_shape=(narrow, narrow, part_shape, part_shape),
        name="local_backward",
        in_specs=[SMEM] + [VMEM] * 12,
        out_specs=(VMEM,) * 4,
        scratch_shapes=[pltpu.VMEM((rows_here, head_dim), jnp.float32)] * 3,
    )(
        table, q, grad, gate, kv_local, key_segments, got, other,
        local_out, local_lse, out, lse, dscore,
    )
    swapped = lax.ppermute(given, "c", SWAP)
    own_sum = kept.astype(jnp.float32) + swapped.astype(jnp.float32)

    arrived = jnp.where(c == 0, stay, back_back)
    arrived = jnp.where(scalar[ARRIVAL] == 2, far_or_next_back, arrived)
    arrived = jnp.where(scalar[ARRIVAL] == 0, jnp.zeros((), arrived.dtype), arrived)
    keep_row = (c * PMAX).astype(jnp.uint32)
    kept_prompt = lax.dynamic_slice(arrived, (keep_row, zero), (PMAX, head_dim))
    given_prompt = lax.dynamic_slice(arrived, (PMAX - keep_row, zero), (PMAX, head_dim))
    swapped_prompt = lax.ppermute(given_prompt, "c", SWAP)
    prompt_rows = (
        own_sum[:PMAX] + kept_prompt.astype(jnp.float32) + swapped_prompt.astype(jnp.float32)
    )
    kv_result = lax.dynamic_update_slice(
        own_sum.astype(jnp.bfloat16), prompt_rows.astype(jnp.bfloat16), (0, 0)
    )
    return (
        attention.reshape(queries.shape), query_gradient.reshape(queries.shape), kv_result
    )


def solution(mesh):
    fine = Mesh(mesh.devices.reshape(NY, NW, NX, NH, NC), ("y", "w", "x", "h", "c"))
    seq, head = ("y", "w", "x"), ("h", "c")
    in_specs = (
        P(seq, head, None),
        P(seq, None, None, None),
        P(seq, head, None),
        P(seq),
        P(),
        P(),
    )
    out_specs = (P(seq, head, None), P(seq, head, None), P(seq, head))
    return jax.shard_map(body, mesh=fine, in_specs=in_specs, out_specs=out_specs, check_vma=False)
```

```python
import math

import jax
import jax.numpy as jnp
from jax import lax
from jax.experimental import pallas as pl
from jax.experimental.pallas import tpu as pltpu
from jax.sharding import Mesh
from jax.sharding import PartitionSpec as P

HEADS = 64
KVH = 8
PMAX = 64
BLK = 16

NY, NW, NX, NH, NC = 4, 4, 4, 8, 2


def run_pairs(moves):
    pairs = []
    for w in range(NW):
        for sh, sc, shift, th, tc in moves:
            source = (w * NH + sh) * NC + sc
            target = ((w + shift) % NW * NH + th) * NC + tc
            pairs.append((source, target))
    return pairs


FORWARD_FAR = [(6 + d // 2, d % 2, 2, d, 0) for d in range(4)] + [
    (d // 2 - 2, d % 2, 2, d, 0) for d in range(4, 8)
]
FORWARD_NEXT = [(2 + d // 2, 1 - d % 2, 1, d, 1) for d in range(8)]
FORWARD_BACK = [(d // 2, d % 2, -1, d, 1) for d in range(8)]
BACKWARD_FAR = [(d, 0, 2, d, 0) for d in range(8)]
BACKWARD_NEXT = [(d, 1, 1, d, 1) for d in range(8)]
BACKWARD_BACK = [(d, 1, -1, d, 1) for d in range(8)]
RUN = ("w", "h", "c")
SWAP = [(0, 1), (1, 0)]


SCALE = 1.0 / math.sqrt(128)
LOG_SCALE = SCALE * math.log2(math.e)
MASKED = -1e30
QROWS = 512
PROWS = 256
TILE = 128


LOW, HIGH, LIVE, DIRECT, CORE, SLOT, FIRST, SEND_FAR, SEND_BACK, SEND_STAY, ARRIVAL, BEGIN, END = range(
    13
)


def route(partner_ref, blocks_ref, segments_ref, table_ref):
    y, w, x = lax.axis_index("y"), lax.axis_index("w"), lax.axis_index("x")
    c = lax.axis_index("c")
    here = y * 16 + w * 4 + x
    owner = partner_ref[here]
    owner_w = (owner >> 2) & 3

    def seek(index, carry):
        far, back, stay, responder = carry
        mark = partner_ref[index]
        shift = (((mark >> 2) & 3) - w) & 3
        in_column = ((mark >> 4) == y) & ((mark & 3) == x)
        slot = ((index >> 4) << 2) | (index & 3)
        far = jnp.where(in_column & (shift == jnp.where(c == 0, 2, 1)), slot, far)
        back = jnp.where(in_column & (shift == 3), slot, back)
        stay = jnp.where(in_column & (shift == 0), slot, stay)
        return far, back, stay, jnp.where(mark == here, index, responder)

    zero = jnp.int32(0)
    far, back, stay, responder = lax.fori_loop(
        0, NY * NW * NX, seek, (zero, zero, zero, zero), unroll=8
    )
    first = zero
    for slot in range(NY * NX):
        wanted = partner_ref[(slot // NX) * 16 + w * 4 + slot % NX]
        first = first | jnp.where((((wanted >> 2) & 3) - w) & 3 < 2, 1 << slot, 0)
    segments = segments_ref[...]
    first_token = jnp.sum((segments < 1).astype(jnp.float32)).astype(jnp.int32)
    end_token = jnp.sum((segments < 2).astype(jnp.float32)).astype(jnp.int32)
    rel = (((responder >> 2) & 3) - w) & 3
    table_ref[LOW] = jnp.minimum(first_token >> 6, 7)
    table_ref[HIGH] = (end_token + 63) >> 6
    table_ref[BEGIN] = first_token
    table_ref[END] = end_token
    table_ref[LIVE] = BLK * blocks_ref[owner]
    table_ref[DIRECT] = (((owner_w - w) & 1) == c).astype(jnp.int32)
    table_ref[CORE] = c
    table_ref[SLOT] = ((owner >> 4) << 2) | (owner & 3)
    table_ref[FIRST] = first
    table_ref[SEND_FAR] = far
    table_ref[SEND_BACK] = back
    table_ref[SEND_STAY] = stay
    table_ref[ARRIVAL] = jnp.where((rel & 1) == c, jnp.where(rel < 2, 1, 2), 0)


def dot(left, right, left_dim, right_dim):
    return lax.dot_general(
        left, right, (((left_dim,), (right_dim,)), ((), ())), preferred_element_type=jnp.float32
    )


def local_scores(q, gate, keys, key_segments, step):
    width = TILE * (step + 1)
    scores = dot(q, keys[:width], 1, 1) + dot(gate, key_segments[:width], 1, 1)
    shape = (QROWS, TILE)
    token = lax.broadcasted_iota(jnp.int32, shape, 0) // 4
    causal = lax.broadcasted_iota(jnp.int32, shape, 1) <= token
    last = jnp.where(causal, scores[:, width - TILE :], MASKED)
    if step == 0:
        return last
    return jnp.concatenate([scores[:, : width - TILE], last], axis=1)


def local_forward(q_ref, gate_ref, kv_ref, keyseg_ref, out_ref, lse_ref):
    for step in range(4):
        rows = pl.ds(step * QROWS, QROWS)
        width = TILE * (step + 1)
        scores = local_scores(q_ref[rows, :], gate_ref[rows, :], kv_ref[0], keyseg_ref[...], step)
        peak = jnp.max(scores, axis=1, keepdims=True)
        weights = jnp.exp2((scores - peak) * LOG_SCALE)
        total = jnp.sum(weights, axis=1, keepdims=True)
        mixed = dot(weights.astype(jnp.bfloat16), kv_ref[1, :width, :], 1, 0)
        out_ref[rows, :] = mixed / total
        lse_ref[rows, :] = jnp.broadcast_to(peak * LOG_SCALE + jnp.log2(total), (QROWS, TILE))


def pick(scalars_ref, got_ref, other_ref):
    return jnp.where(scalars_ref[DIRECT] == 1, got_ref[...], other_ref[...])


def prompt_step(
    scalars_ref, got_ref, other_ref, q_ref, grad_ref, outin_ref, lsein_ref,
    dprompt_ref, out_ref, lse_ref, dscore_ref,
    qbuf_ref, gradbuf_ref, outbuf_ref, lsebuf_ref, outnew_ref, lsenew_ref, dscorenew_ref,
    insems_ref, outsems_ref, dkey_ref, dvalue_ref,
):
    low_block, high_block = scalars_ref[LOW], scalars_ref[HIGH]
    coming = ((q_ref, qbuf_ref), (grad_ref, gradbuf_ref), (outin_ref, outbuf_ref), (lsein_ref, lsebuf_ref))
    leaving = ((out_ref, outnew_ref), (lse_ref, lsenew_ref), (dscore_ref, dscorenew_ref))

    def loads(index, slot):
        rows = pl.ds(pl.multiple_of(index * PROWS, PROWS), PROWS)
        return [
            pltpu.make_async_copy(far.at[rows, :], buffer.at[slot], insems_ref.at[k, slot])
            for k, (far, buffer) in enumerate(coming)
        ]

    def stores(index, slot):
        rows = pl.ds(pl.multiple_of(index * PROWS, PROWS), PROWS)
        return [
            pltpu.make_async_copy(buffer.at[slot], far.at[rows, :], outsems_ref.at[k, slot])
            for k, (far, buffer) in enumerate(leaving)
        ]

    for copy in loads(low_block, 0):
        copy.start()
    prompt = pick(scalars_ref, got_ref, other_ref)
    keys, values = prompt[:PMAX], prompt[PMAX:]
    alive = lax.broadcasted_iota(jnp.int32, (PROWS, PMAX), 1) < scalars_ref[LIVE]
    row = lax.broadcasted_iota(jnp.int32, (PROWS, PMAX), 0)
    dkey_ref[...] = jnp.zeros_like(dkey_ref)
    dvalue_ref[...] = jnp.zeros_like(dvalue_ref)

    def block(index, carry):
        slot = (index - low_block) & 1

        @pl.when(index + 1 < high_block)
        def _():
            for copy in loads(index + 1, 1 - slot):
                copy.start()

        for copy in loads(index, slot):
            copy.wait()

        @pl.when(index >= low_block + 2)
        def _():
            for copy in stores(index - 2, slot):
                copy.wait()

        first_row = index * PROWS
        q, grad = qbuf_ref[slot], gradbuf_ref[slot]
        allowed = (
            alive
            & (row >= 4 * scalars_ref[BEGIN] - first_row)
            & (row < 4 * scalars_ref[END] - first_row)
        )
        logits = jnp.where(allowed, dot(q, keys, 1, 1), MASKED) * LOG_SCALE
        lse = lsebuf_ref[slot][:, :1]
        peak = jnp.maximum(lse, jnp.max(logits, axis=1, keepdims=True))
        weights = jnp.exp2(logits - peak)
        before = jnp.exp2(lse - peak)
        total = before + jnp.sum(weights, axis=1, keepdims=True)
        inverse = 1.0 / total
        probabilities = weights * inverse
        low = probabilities.astype(jnp.bfloat16)
        out = outbuf_ref[slot] * (before * inverse) + dot(low, values, 1, 0)
        outnew_ref[slot] = out
        lsenew_ref[slot] = jnp.broadcast_to(peak + jnp.log2(total), (PROWS, TILE))
        rounded = out.astype(jnp.bfloat16).astype(jnp.float32)
        delta = jnp.sum(grad.astype(jnp.float32) * rounded, axis=1, keepdims=True)
        dscore = (probabilities * (dot(grad, values, 1, 1) - delta)).astype(jnp.bfloat16)
        dscorenew_ref[slot, :, :PMAX] = dscore
        for copy in stores(index, slot):
            copy.start()
        dvalue_ref[...] += dot(low, grad, 0, 0)
        dkey_ref[...] += dot(dscore, q, 0, 0)
        return carry

    lax.fori_loop(low_block, high_block, block, 0)
    dprompt_ref[:PMAX, :] = (dkey_ref[...] * SCALE).astype(jnp.bfloat16)
    dprompt_ref[PMAX:, :] = dvalue_ref[...].astype(jnp.bfloat16)
    for back in (2, 1):
        @pl.when(high_block - back >= low_block)
        def _():
            for copy in stores(high_block - back, (high_block - back - low_block) & 1):
                copy.wait()


def local_backward(
    scalars_ref, q_ref, grad_ref, gate_ref, kv_ref, keyseg_ref, got_ref, other_ref,
    outlocal_ref, lselocal_ref, outprompt_ref, lseprompt_ref, dscore_ref,
    attention_ref, dquery_ref, kept_ref, given_ref, dkey_ref, dvalue_ref, acc_ref,
):
    def chosen(prompt_ref, local_ref, step):
        parts = []
        for part in range(QROWS // PROWS):
            index = step * (QROWS // PROWS) + part
            inside = (scalars_ref[LOW] <= index) & (index < scalars_ref[HIGH])
            rows = pl.ds(index * PROWS, PROWS)
            parts.append(jnp.where(inside, prompt_ref[rows, :], local_ref[rows, :]))
        return jnp.concatenate(parts, axis=0)

    dkey_ref[...] = jnp.zeros_like(dkey_ref)
    dvalue_ref[...] = jnp.zeros_like(dvalue_ref)
    prompt_keys = pick(scalars_ref, got_ref, other_ref)[:PMAX]
    for step in range(4):
        rows = pl.ds(step * QROWS, QROWS)
        width = TILE * (step + 1)
        q, grad = q_ref[rows, :], grad_ref[rows, :]
        attention = chosen(outprompt_ref, outlocal_ref, step).astype(jnp.bfloat16)
        attention_ref[rows, :] = attention
        delta = jnp.sum(
            grad.astype(jnp.float32) * attention.astype(jnp.float32), axis=1, keepdims=True
        )
        scores = local_scores(q, gate_ref[rows, :], kv_ref[0], keyseg_ref[...], step)
        lse = chosen(lseprompt_ref, lselocal_ref, step)
        if step:
            lse = jnp.concatenate([lse] * (step + 1), axis=1)
        probabilities = jnp.exp2(scores * LOG_SCALE - lse)
        low = probabilities.astype(jnp.bfloat16)
        dprob = dot(grad, kv_ref[1, :width, :], 1, 1)
        dscore = (probabilities * (dprob - delta)).astype(jnp.bfloat16)
        acc_ref[...] = dot(dscore, kv_ref[0, :width, :], 1, 0)
        dvalue_ref[:width, :] += dot(low, grad, 0, 0)
        dkey_ref[:width, :] += dot(dscore, q, 0, 0)
        for part in range(QROWS // PROWS):
            index = step * (QROWS // PROWS) + part

            @pl.when((scalars_ref[LOW] <= index) & (index < scalars_ref[HIGH]))
            def _():
                acc_ref[pl.ds(part * PROWS, PROWS), :] += dot(
                    dscore_ref[pl.ds(index * PROWS, PROWS), :PMAX], prompt_keys, 1, 0
                )

        dquery_ref[rows, :] = (acc_ref[...] * SCALE).astype(jnp.bfloat16)
    dkey = dkey_ref[...] * SCALE
    dvalue = dvalue_ref[...]
    keep_key = scalars_ref[CORE] == 0
    kept_ref[...] = jnp.where(keep_key, dkey, dvalue).astype(jnp.bfloat16)
    given_ref[...] = jnp.where(keep_key, dvalue, dkey).astype(jnp.bfloat16)


SMEM = pl.BlockSpec(memory_space=pltpu.SMEM)
VMEM = pl.BlockSpec(memory_space=pltpu.VMEM)
FAR = pl.BlockSpec(memory_space=pltpu.HBM)


def near(array):
    return pltpu.with_memory_space_constraint(array, pltpu.VMEM)


def body(queries, keys_values, grad_out, segments, partner, prompt_blocks):
    rows_here = queries.shape[0]
    heads_here = queries.shape[1]
    head_dim = queries.shape[2]
    flat = rows_here * heads_here
    y, w, x = lax.axis_index("y"), lax.axis_index("w"), lax.axis_index("x")
    h, c = lax.axis_index("h"), lax.axis_index("c")

    zero = jnp.uint32(0)

    def prompt_of(head):
        rows = lax.dynamic_slice(
            keys_values, (zero, zero, head.astype(jnp.uint32), zero), (PMAX, 2, 1, head_dim)
        )
        return jnp.transpose(rows[:, :, 0], (1, 0, 2)).reshape(2 * PMAX, head_dim)

    far_sender = (h < 2) | (h >= 6)
    head_far = jnp.where(h < 2, 2 * h + c + 4, 2 * h + c - 12)
    head_next = 2 * h + 1 - c - 4
    far_or_next = lax.ppermute(
        prompt_of(jnp.where(far_sender, head_far, head_next)), RUN,
        run_pairs(FORWARD_FAR + FORWARD_NEXT),
    )
    back = lax.ppermute(
        prompt_of((2 * h + c) & (NH - 1)), RUN, run_pairs(FORWARD_BACK)
    )
    own = prompt_of(h)

    table = pl.pallas_call(
        route, out_shape=jax.ShapeDtypeStruct((16,), jnp.int32), name="route",
        in_specs=[SMEM, SMEM, VMEM], out_specs=SMEM,
    )(partner, prompt_blocks, segments.reshape(-1, TILE))

    kv_local = jnp.transpose(
        lax.dynamic_index_in_dim(keys_values, h.astype(jnp.uint32), 2, keepdims=False), (1, 0, 2)
    )
    lanes = jnp.arange(TILE, dtype=jnp.int32)
    row_segments = jnp.broadcast_to(segments[:, None], (rows_here, heads_here)).reshape(flat)
    gate = jnp.where(row_segments[:, None] == lanes[None, :], 0.0, MASKED).astype(jnp.bfloat16)
    key_segments = (segments[:, None] == lanes[None, :]).astype(jnp.bfloat16)
    q = queries.reshape(flat, head_dim)
    grad = grad_out.reshape(flat, head_dim)

    wide = pltpu.HBM((flat, head_dim), jnp.float32)
    narrow = jax.ShapeDtypeStruct((flat, head_dim), jnp.bfloat16)
    part_shape = jax.ShapeDtypeStruct((rows_here, head_dim), jnp.bfloat16)
    scalar = [table[k].astype(jnp.uint32) for k in range(11)]

    slots = jnp.arange(NY * NX, dtype=jnp.uint32)
    first = jnp.where(c == 0, own, back)
    take_first = (scalar[FIRST] >> slots) & 1 == 1
    outgoing = jnp.where(take_first[:, None, None], first[None], far_or_next[None])
    outgoing, kv_local, gate, key_segments, scalar = lax.optimization_barrier(
        (outgoing, kv_local, gate, key_segments, scalar)
    )
    incoming = lax.all_to_all(outgoing, ("y", "x"), split_axis=0, concat_axis=0, tiled=True)
    local_out, local_lse = pl.pallas_call(
        local_forward, out_shape=(wide, wide), name="local_forward",
        in_specs=[VMEM] * 4, out_specs=(VMEM, VMEM),
    )(q, gate, kv_local, key_segments)
    incoming, local_out, local_lse = lax.optimization_barrier((incoming, local_out, local_lse))
    got = lax.dynamic_index_in_dim(incoming, scalar[SLOT], 0, keepdims=False)
    other = lax.ppermute(got, "c", SWAP)

    dprompt, out, lse, dscore = pl.pallas_call(
        prompt_step,
        out_shape=(
            pltpu.VMEM((2 * PMAX, head_dim), jnp.bfloat16), wide, wide,
            pltpu.HBM((flat, TILE), jnp.bfloat16),
        ),
        in_specs=[SMEM, VMEM, VMEM] + [FAR] * 4,
        out_specs=(VMEM, FAR, FAR, FAR),
        scratch_shapes=(
            [pltpu.VMEM((2, PROWS, head_dim), jnp.bfloat16)] * 2
            + [pltpu.VMEM((2, PROWS, head_dim), jnp.float32)] * 4
            + [pltpu.VMEM((2, PROWS, TILE), jnp.bfloat16)]
            + [pltpu.SemaphoreType.DMA((4, 2)), pltpu.SemaphoreType.DMA((3, 2))]
            + [pltpu.VMEM((PMAX, head_dim), jnp.float32)] * 2
        ),
        name="prompt_step",
    )(table, near(got), near(other), q, grad, local_out, local_lse)

    total = dprompt.astype(jnp.float32) + lax.ppermute(dprompt, "c", SWAP).astype(jnp.float32)
    spread = jnp.where(
        (slots == scalar[SLOT])[:, None, None], total.astype(jnp.bfloat16)[None],
        jnp.zeros((), jnp.bfloat16),
    )
    spread = lax.all_to_all(spread, ("y", "x"), split_axis=0, concat_axis=0, tiled=True)

    def parcel(slot):
        return lax.dynamic_index_in_dim(spread, slot, 0, keepdims=False)

    far_or_next_back = lax.ppermute(
        parcel(scalar[SEND_FAR]), RUN, run_pairs(BACKWARD_FAR + BACKWARD_NEXT)
    )
    back_back = lax.ppermute(parcel(scalar[SEND_BACK]), RUN, run_pairs(BACKWARD_BACK))
    stay = parcel(scalar[SEND_STAY])

    attention, query_gradient, kept, given = pl.pallas_call(
        local_backward,
        out_shape=(narrow, narrow, part_shape, part_shape),
        name="local_backward",
        in_specs=[SMEM] + [VMEM] * 12,
        out_specs=(VMEM,) * 4,
        scratch_shapes=[pltpu.VMEM((rows_here, head_dim), jnp.float32)] * 3,
    )(
        table, q, grad, gate, kv_local, key_segments, got, other,
        local_out, local_lse, out, lse, dscore,
    )
    swapped = lax.ppermute(given, "c", SWAP)
    own_sum = kept.astype(jnp.float32) + swapped.astype(jnp.float32)

    arrived = jnp.where(c == 0, stay, back_back)
    arrived = jnp.where(scalar[ARRIVAL] == 2, far_or_next_back, arrived)
    arrived = jnp.where(scalar[ARRIVAL] == 0, jnp.zeros((), arrived.dtype), arrived)
    keep_row = (c * PMAX).astype(jnp.uint32)
    kept_prompt = lax.dynamic_slice(arrived, (keep_row, zero), (PMAX, head_dim))
    given_prompt = lax.dynamic_slice(arrived, (PMAX - keep_row, zero), (PMAX, head_dim))
    swapped_prompt = lax.ppermute(given_prompt, "c", SWAP)
    prompt_rows = (
        own_sum[:PMAX] + kept_prompt.astype(jnp.float32) + swapped_prompt.astype(jnp.float32)
    )
    kv_result = lax.dynamic_update_slice(
        own_sum.astype(jnp.bfloat16), prompt_rows.astype(jnp.bfloat16), (0, 0)
    )
    return (
        attention.reshape(queries.shape), query_gradient.reshape(queries.shape), kv_result
    )


def solution(mesh):
    fine = Mesh(mesh.devices.reshape(NY, NW, NX, NH, NC), ("y", "w", "x", "h", "c"))
    seq, head = ("y", "w", "x"), ("h", "c")
    in_specs = (
        P(seq, head, None),
        P(seq, None, None, None),
        P(seq, head, None),
        P(seq),
        P(),
        P(),
    )
    out_specs = (P(seq, head, None), P(seq, head, None), P(seq, head))
    return jax.shard_map(body, mesh=fine, in_specs=in_specs, out_specs=out_specs, check_vma=False)
```

```python
import math

import jax
import jax.numpy as jnp
from jax import lax
from jax.experimental import pallas as pl
from jax.experimental.pallas import tpu as pltpu
from jax.sharding import Mesh
from jax.sharding import PartitionSpec as P

HEADS = 64
KVH = 8
PMAX = 64
BLK = 16

NY, NW, NX, NH, NC = 4, 4, 4, 8, 2


def run_pairs(moves):
    pairs = []
    for w in range(NW):
        for sh, sc, shift, th, tc in moves:
            source = (w * NH + sh) * NC + sc
            target = ((w + shift) % NW * NH + th) * NC + tc
            pairs.append((source, target))
    return pairs


FORWARD_FAR = [(6 + d // 2, d % 2, 2, d, 0) for d in range(4)] + [
    (d // 2 - 2, d % 2, 2, d, 0) for d in range(4, 8)
]
FORWARD_NEXT = [(2 + d // 2, 1 - d % 2, 1, d, 1) for d in range(8)]
FORWARD_BACK = [(d // 2, d % 2, -1, d, 1) for d in range(8)]
BACKWARD_FAR = [(d, 0, 2, d, 0) for d in range(8)]
BACKWARD_NEXT = [(d, 1, 1, d, 1) for d in range(8)]
BACKWARD_BACK = [(d, 1, -1, d, 1) for d in range(8)]
RUN = ("w", "h", "c")
SWAP = [(0, 1), (1, 0)]


SCALE = 1.0 / math.sqrt(128)
LOG_SCALE = SCALE * math.log2(math.e)
MASKED = -1e30
QROWS = 512
PROWS = 256
TILE = 128


LOW, HIGH, LIVE, DIRECT, CORE, BEGIN, END = range(7)


def route(
    partner_ref, blocks_ref, segments_ref,
    table_ref, slot_ref, first_ref, far_ref, back_ref, stay_ref, arrival_ref,
):
    y, w, x = lax.axis_index("y"), lax.axis_index("w"), lax.axis_index("x")
    c = lax.axis_index("c")
    here = y * 16 + w * 4 + x
    owner = partner_ref[here]
    owner_w = (owner >> 2) & 3

    def seek(index, carry):
        far, back, stay, responder = carry
        mark = partner_ref[index]
        shift = (((mark >> 2) & 3) - w) & 3
        in_column = ((mark >> 4) == y) & ((mark & 3) == x)
        slot = ((index >> 4) << 2) | (index & 3)
        far = jnp.where(in_column & (shift == jnp.where(c == 0, 2, 1)), slot, far)
        back = jnp.where(in_column & (shift == 3), slot, back)
        stay = jnp.where(in_column & (shift == 0), slot, stay)
        return far, back, stay, jnp.where(mark == here, index, responder)

    zero = jnp.int32(0)
    far, back, stay, responder = lax.fori_loop(
        0, NY * NW * NX, seek, (zero, zero, zero, zero), unroll=8
    )
    first = zero
    for slot in range(NY * NX):
        wanted = partner_ref[(slot // NX) * 16 + w * 4 + slot % NX]
        first = first | jnp.where((((wanted >> 2) & 3) - w) & 3 < 2, 1 << slot, 0)
    segments = segments_ref[...]
    first_token = jnp.sum((segments < 1).astype(jnp.float32)).astype(jnp.int32)
    end_token = jnp.sum((segments < 2).astype(jnp.float32)).astype(jnp.int32)
    rel = (((responder >> 2) & 3) - w) & 3
    table_ref[LOW] = jnp.minimum(first_token >> 6, 7)
    table_ref[HIGH] = (end_token + 63) >> 6
    table_ref[BEGIN] = first_token
    table_ref[END] = end_token
    table_ref[LIVE] = BLK * blocks_ref[owner]
    table_ref[DIRECT] = (((owner_w - w) & 1) == c).astype(jnp.int32)
    table_ref[CORE] = c
    arrival = jnp.where((rel & 1) == c, jnp.where(rel < 2, 1, 2), 0)
    slot_ref[0] = (((owner >> 4) << 2) | (owner & 3)).astype(jnp.uint32)
    first_ref[0] = first.astype(jnp.uint32)
    far_ref[0] = far.astype(jnp.uint32)
    back_ref[0] = back.astype(jnp.uint32)
    stay_ref[0] = stay.astype(jnp.uint32)
    arrival_ref[0] = arrival.astype(jnp.uint32)


def dot(left, right, left_dim, right_dim):
    return lax.dot_general(
        left, right, (((left_dim,), (right_dim,)), ((), ())), preferred_element_type=jnp.float32
    )


def local_scores(q, gate, keys, key_segments, step):
    width = TILE * (step + 1)
    scores = dot(q, keys[:width], 1, 1) + dot(gate, key_segments[:width], 1, 1)
    shape = (QROWS, TILE)
    token = lax.broadcasted_iota(jnp.int32, shape, 0) // 4
    causal = lax.broadcasted_iota(jnp.int32, shape, 1) <= token
    last = jnp.where(causal, scores[:, width - TILE :], MASKED)
    if step == 0:
        return last
    return jnp.concatenate([scores[:, : width - TILE], last], axis=1)


def local_forward(q_ref, gate_ref, kv_ref, keyseg_ref, out_ref, lse_ref):
    for step in range(4):
        rows = pl.ds(step * QROWS, QROWS)
        width = TILE * (step + 1)
        scores = local_scores(q_ref[rows, :], gate_ref[rows, :], kv_ref[0], keyseg_ref[...], step)
        peak = jnp.max(scores, axis=1, keepdims=True)
        weights = jnp.exp2((scores - peak) * LOG_SCALE)
        total = jnp.sum(weights, axis=1, keepdims=True)
        mixed = dot(weights.astype(jnp.bfloat16), kv_ref[1, :width, :], 1, 0)
        out_ref[rows, :] = mixed / total
        lse_ref[rows, :] = jnp.broadcast_to(peak * LOG_SCALE + jnp.log2(total), (QROWS, TILE))


def pick(scalars_ref, got_ref, other_ref):
    return jnp.where(scalars_ref[DIRECT] == 1, got_ref[...], other_ref[...])


def prompt_step(
    scalars_ref, got_ref, other_ref, q_ref, grad_ref, outin_ref, lsein_ref,
    dprompt_ref, out_ref, lse_ref, dscore_ref,
    qbuf_ref, gradbuf_ref, outbuf_ref, lsebuf_ref, outnew_ref, lsenew_ref, dscorenew_ref,
    insems_ref, outsems_ref, dkey_ref, dvalue_ref,
):
    low_block, high_block = scalars_ref[LOW], scalars_ref[HIGH]
    coming = ((q_ref, qbuf_ref), (grad_ref, gradbuf_ref), (outin_ref, outbuf_ref), (lsein_ref, lsebuf_ref))
    leaving = ((out_ref, outnew_ref), (lse_ref, lsenew_ref), (dscore_ref, dscorenew_ref))

    def loads(index, slot):
        rows = pl.ds(pl.multiple_of(index * PROWS, PROWS), PROWS)
        return [
            pltpu.make_async_copy(far.at[rows, :], buffer.at[slot], insems_ref.at[k, slot])
            for k, (far, buffer) in enumerate(coming)
        ]

    def stores(index, slot):
        rows = pl.ds(pl.multiple_of(index * PROWS, PROWS), PROWS)
        return [
            pltpu.make_async_copy(buffer.at[slot], far.at[rows, :], outsems_ref.at[k, slot])
            for k, (far, buffer) in enumerate(leaving)
        ]

    for copy in loads(low_block, 0):
        copy.start()
    prompt = pick(scalars_ref, got_ref, other_ref)
    keys, values = prompt[:PMAX], prompt[PMAX:]
    alive = lax.broadcasted_iota(jnp.int32, (PROWS, PMAX), 1) < scalars_ref[LIVE]
    row = lax.broadcasted_iota(jnp.int32, (PROWS, PMAX), 0)
    dkey_ref[...] = jnp.zeros_like(dkey_ref)
    dvalue_ref[...] = jnp.zeros_like(dvalue_ref)

    def block(index, carry):
        slot = (index - low_block) & 1

        @pl.when(index + 1 < high_block)
        def _():
            for copy in loads(index + 1, 1 - slot):
                copy.start()

        for copy in loads(index, slot):
            copy.wait()

        @pl.when(index >= low_block + 2)
        def _():
            for copy in stores(index - 2, slot):
                copy.wait()

        first_row = index * PROWS
        q, grad = qbuf_ref[slot], gradbuf_ref[slot]
        allowed = (
            alive
            & (row >= 4 * scalars_ref[BEGIN] - first_row)
            & (row < 4 * scalars_ref[END] - first_row)
        )
        logits = jnp.where(allowed, dot(q, keys, 1, 1), MASKED) * LOG_SCALE
        lse = lsebuf_ref[slot][:, :1]
        peak = jnp.maximum(lse, jnp.max(logits, axis=1, keepdims=True))
        weights = jnp.exp2(logits - peak)
        before = jnp.exp2(lse - peak)
        total = before + jnp.sum(weights, axis=1, keepdims=True)
        inverse = 1.0 / total
        probabilities = weights * inverse
        low = probabilities.astype(jnp.bfloat16)
        out = outbuf_ref[slot] * (before * inverse) + dot(low, values, 1, 0)
        outnew_ref[slot] = out
        lsenew_ref[slot] = jnp.broadcast_to(peak + jnp.log2(total), (PROWS, TILE))
        rounded = out.astype(jnp.bfloat16).astype(jnp.float32)
        delta = jnp.sum(grad.astype(jnp.float32) * rounded, axis=1, keepdims=True)
        dscore = (probabilities * (dot(grad, values, 1, 1) - delta)).astype(jnp.bfloat16)
        dscorenew_ref[slot, :, :PMAX] = dscore
        for copy in stores(index, slot):
            copy.start()
        dvalue_ref[...] += dot(low, grad, 0, 0)
        dkey_ref[...] += dot(dscore, q, 0, 0)
        return carry

    lax.fori_loop(low_block, high_block, block, 0)
    dprompt_ref[:PMAX, :] = (dkey_ref[...] * SCALE).astype(jnp.bfloat16)
    dprompt_ref[PMAX:, :] = dvalue_ref[...].astype(jnp.bfloat16)
    for back in (2, 1):
        @pl.when(high_block - back >= low_block)
        def _():
            for copy in stores(high_block - back, (high_block - back - low_block) & 1):
                copy.wait()


def local_backward(
    scalars_ref, q_ref, grad_ref, gate_ref, kv_ref, keyseg_ref, got_ref, other_ref,
    outlocal_ref, lselocal_ref, outprompt_ref, lseprompt_ref, dscore_ref,
    attention_ref, dquery_ref, kept_ref, given_ref, dkey_ref, dvalue_ref, acc_ref,
):
    def chosen(prompt_ref, local_ref, step):
        parts = []
        for part in range(QROWS // PROWS):
            index = step * (QROWS // PROWS) + part
            inside = (scalars_ref[LOW] <= index) & (index < scalars_ref[HIGH])
            rows = pl.ds(index * PROWS, PROWS)
            parts.append(jnp.where(inside, prompt_ref[rows, :], local_ref[rows, :]))
        return jnp.concatenate(parts, axis=0)

    dkey_ref[...] = jnp.zeros_like(dkey_ref)
    dvalue_ref[...] = jnp.zeros_like(dvalue_ref)
    prompt_keys = pick(scalars_ref, got_ref, other_ref)[:PMAX]
    for step in range(4):
        rows = pl.ds(step * QROWS, QROWS)
        width = TILE * (step + 1)
        q, grad = q_ref[rows, :], grad_ref[rows, :]
        attention = chosen(outprompt_ref, outlocal_ref, step).astype(jnp.bfloat16)
        attention_ref[rows, :] = attention
        delta = jnp.sum(
            grad.astype(jnp.float32) * attention.astype(jnp.float32), axis=1, keepdims=True
        )
        scores = local_scores(q, gate_ref[rows, :], kv_ref[0], keyseg_ref[...], step)
        lse = chosen(lseprompt_ref, lselocal_ref, step)
        if step:
            lse = jnp.concatenate([lse] * (step + 1), axis=1)
        probabilities = jnp.exp2(scores * LOG_SCALE - lse)
        low = probabilities.astype(jnp.bfloat16)
        dprob = dot(grad, kv_ref[1, :width, :], 1, 1)
        dscore = (probabilities * (dprob - delta)).astype(jnp.bfloat16)
        acc_ref[...] = dot(dscore, kv_ref[0, :width, :], 1, 0)
        dvalue_ref[:width, :] += dot(low, grad, 0, 0)
        dkey_ref[:width, :] += dot(dscore, q, 0, 0)
        for part in range(QROWS // PROWS):
            index = step * (QROWS // PROWS) + part

            @pl.when((scalars_ref[LOW] <= index) & (index < scalars_ref[HIGH]))
            def _():
                acc_ref[pl.ds(part * PROWS, PROWS), :] += dot(
                    dscore_ref[pl.ds(index * PROWS, PROWS), :PMAX], prompt_keys, 1, 0
                )

        dquery_ref[rows, :] = (acc_ref[...] * SCALE).astype(jnp.bfloat16)
    dkey = dkey_ref[...] * SCALE
    dvalue = dvalue_ref[...]
    keep_key = scalars_ref[CORE] == 0
    kept_ref[...] = jnp.where(keep_key, dkey, dvalue).astype(jnp.bfloat16)
    given_ref[...] = jnp.where(keep_key, dvalue, dkey).astype(jnp.bfloat16)


SMEM = pl.BlockSpec(memory_space=pltpu.SMEM)
VMEM = pl.BlockSpec(memory_space=pltpu.VMEM)
FAR = pl.BlockSpec(memory_space=pltpu.HBM)


def near(array):
    return pltpu.with_memory_space_constraint(array, pltpu.VMEM)


def body(queries, keys_values, grad_out, segments, partner, prompt_blocks):
    rows_here = queries.shape[0]
    heads_here = queries.shape[1]
    head_dim = queries.shape[2]
    flat = rows_here * heads_here
    y, w, x = lax.axis_index("y"), lax.axis_index("w"), lax.axis_index("x")
    h, c = lax.axis_index("h"), lax.axis_index("c")

    zero = jnp.uint32(0)

    def prompt_of(head):
        rows = lax.dynamic_slice(
            keys_values, (zero, zero, head.astype(jnp.uint32), zero), (PMAX, 2, 1, head_dim)
        )
        return jnp.transpose(rows[:, :, 0], (1, 0, 2)).reshape(2 * PMAX, head_dim)

    far_sender = (h < 2) | (h >= 6)
    head_far = jnp.where(h < 2, 2 * h + c + 4, 2 * h + c - 12)
    head_next = 2 * h + 1 - c - 4
    far_or_next = lax.ppermute(
        prompt_of(jnp.where(far_sender, head_far, head_next)), RUN,
        run_pairs(FORWARD_FAR + FORWARD_NEXT),
    )
    back = lax.ppermute(
        prompt_of((2 * h + c) & (NH - 1)), RUN, run_pairs(FORWARD_BACK)
    )
    own = prompt_of(h)

    one = jax.ShapeDtypeStruct((1,), jnp.uint32)
    table, *scalar = pl.pallas_call(
        route, out_shape=(jax.ShapeDtypeStruct((16,), jnp.int32),) + (one,) * 6, name="route",
        in_specs=[SMEM, SMEM, VMEM], out_specs=(SMEM,) * 7,
    )(partner, prompt_blocks, segments.reshape(-1, TILE))
    to_slot, first_bits, far_slot, back_slot, stay_slot, arrival = (s.reshape(()) for s in scalar)

    kv_mixed = lax.dynamic_index_in_dim(keys_values, h.astype(jnp.uint32), 2, keepdims=False)
    lanes = jnp.arange(TILE, dtype=jnp.int32)
    key_segments = (segments[:, None] == lanes[None, :]).astype(jnp.bfloat16)
    q = queries.reshape(flat, head_dim)
    grad = grad_out.reshape(flat, head_dim)

    wide = pltpu.HBM((flat, head_dim), jnp.float32)
    narrow = jax.ShapeDtypeStruct((flat, head_dim), jnp.bfloat16)
    part_shape = jax.ShapeDtypeStruct((rows_here, head_dim), jnp.bfloat16)

    slots = jnp.arange(NY * NX, dtype=jnp.uint32)
    first = jnp.where(c == 0, own, back)
    take_first = (first_bits >> slots) & 1 == 1
    outgoing = jnp.where(take_first[:, None, None], first[None], far_or_next[None])
    outgoing, kv_mixed, key_segments, segments = lax.optimization_barrier(
        (outgoing, kv_mixed, key_segments, segments)
    )
    kv_local = jnp.transpose(kv_mixed, (1, 0, 2))
    row_segments = jnp.broadcast_to(segments[:, None], (rows_here, heads_here)).reshape(flat)
    gate = jnp.where(row_segments[:, None] == lanes[None, :], 0.0, MASKED).astype(jnp.bfloat16)
    incoming = lax.all_to_all(outgoing, ("y", "x"), split_axis=0, concat_axis=0, tiled=True)
    local_out, local_lse = pl.pallas_call(
        local_forward, out_shape=(wide, wide), name="local_forward",
        in_specs=[VMEM] * 4, out_specs=(VMEM, VMEM),
    )(q, gate, kv_local, key_segments)
    incoming, local_out, local_lse = lax.optimization_barrier((incoming, local_out, local_lse))
    got = lax.dynamic_index_in_dim(incoming, to_slot, 0, keepdims=False)
    other = lax.ppermute(got, "c", SWAP)

    dprompt, out, lse, dscore = pl.pallas_call(
        prompt_step,
        out_shape=(
            pltpu.VMEM((2 * PMAX, head_dim), jnp.bfloat16), wide, wide,
            pltpu.HBM((flat, TILE), jnp.bfloat16),
        ),
        in_specs=[SMEM, VMEM, VMEM] + [FAR] * 4,
        out_specs=(VMEM, FAR, FAR, FAR),
        scratch_shapes=(
            [pltpu.VMEM((2, PROWS, head_dim), jnp.bfloat16)] * 2
            + [pltpu.VMEM((2, PROWS, head_dim), jnp.float32)] * 4
            + [pltpu.VMEM((2, PROWS, TILE), jnp.bfloat16)]
            + [pltpu.SemaphoreType.DMA((4, 2)), pltpu.SemaphoreType.DMA((3, 2))]
            + [pltpu.VMEM((PMAX, head_dim), jnp.float32)] * 2
        ),
        name="prompt_step",
    )(table, near(got), near(other), q, grad, local_out, local_lse)

    total = dprompt.astype(jnp.float32) + lax.ppermute(dprompt, "c", SWAP).astype(jnp.float32)
    spread = jnp.where(
        (slots == to_slot)[:, None, None], total.astype(jnp.bfloat16)[None],
        jnp.zeros((), jnp.bfloat16),
    )
    spread = lax.all_to_all(spread, ("y", "x"), split_axis=0, concat_axis=0, tiled=True)

    def parcel(slot):
        return lax.dynamic_index_in_dim(spread, slot, 0, keepdims=False)

    far_or_next_back = lax.ppermute(
        parcel(far_slot), RUN, run_pairs(BACKWARD_FAR + BACKWARD_NEXT)
    )
    back_back = lax.ppermute(parcel(back_slot), RUN, run_pairs(BACKWARD_BACK))
    stay = parcel(stay_slot)

    attention, query_gradient, kept, given = pl.pallas_call(
        local_backward,
        out_shape=(narrow, narrow, part_shape, part_shape),
        name="local_backward",
        in_specs=[SMEM] + [VMEM] * 12,
        out_specs=(VMEM,) * 4,
        scratch_shapes=[pltpu.VMEM((rows_here, head_dim), jnp.float32)] * 3,
    )(
        table, q, grad, gate, kv_local, key_segments, got, other,
        local_out, local_lse, out, lse, dscore,
    )
    swapped = lax.ppermute(given, "c", SWAP)
    own_sum = kept.astype(jnp.float32) + swapped.astype(jnp.float32)

    arrived = jnp.where(c == 0, stay, back_back)
    arrived = jnp.where(arrival == 2, far_or_next_back, arrived)
    arrived = jnp.where(arrival == 0, jnp.zeros((), arrived.dtype), arrived)
    keep_row = (c * PMAX).astype(jnp.uint32)
    kept_prompt = lax.dynamic_slice(arrived, (keep_row, zero), (PMAX, head_dim))
    given_prompt = lax.dynamic_slice(arrived, (PMAX - keep_row, zero), (PMAX, head_dim))
    swapped_prompt = lax.ppermute(given_prompt, "c", SWAP)
    prompt_rows = (
        own_sum[:PMAX] + kept_prompt.astype(jnp.float32) + swapped_prompt.astype(jnp.float32)
    )
    kv_result = lax.dynamic_update_slice(
        own_sum.astype(jnp.bfloat16), prompt_rows.astype(jnp.bfloat16), (0, 0)
    )
    return (
        attention.reshape(queries.shape), query_gradient.reshape(queries.shape), kv_result
    )


def solution(mesh):
    fine = Mesh(mesh.devices.reshape(NY, NW, NX, NH, NC), ("y", "w", "x", "h", "c"))
    seq, head = ("y", "w", "x"), ("h", "c")
    in_specs = (
        P(seq, head, None),
        P(seq, None, None, None),
        P(seq, head, None),
        P(seq),
        P(),
        P(),
    )
    out_specs = (P(seq, head, None), P(seq, head, None), P(seq, head))
    return jax.shard_map(body, mesh=fine, in_specs=in_specs, out_specs=out_specs, check_vma=False)
```

```python
import math

import jax
import jax.numpy as jnp
from jax import lax
from jax.experimental import pallas as pl
from jax.experimental.pallas import tpu as pltpu
from jax.sharding import Mesh
from jax.sharding import PartitionSpec as P

HEADS = 64
KVH = 8
PMAX = 64
BLK = 16

NY, NW, NX, NH, NC = 4, 4, 4, 8, 2


def run_pairs(moves):
    pairs = []
    for w in range(NW):
        for sh, sc, shift, th, tc in moves:
            source = (w * NH + sh) * NC + sc
            target = ((w + shift) % NW * NH + th) * NC + tc
            pairs.append((source, target))
    return pairs


FORWARD_FAR = [(6 + d // 2, d % 2, 2, d, 0) for d in range(4)] + [
    (d // 2 - 2, d % 2, 2, d, 0) for d in range(4, 8)
]
FORWARD_NEXT = [(2 + d // 2, 1 - d % 2, 1, d, 1) for d in range(8)]
FORWARD_BACK = [(d // 2, d % 2, -1, d, 1) for d in range(8)]
BACKWARD_FAR = [(d, 0, 2, d, 0) for d in range(8)]
BACKWARD_NEXT = [(d, 1, 1, d, 1) for d in range(8)]
BACKWARD_BACK = [(d, 1, -1, d, 1) for d in range(8)]
RUN = ("w", "h", "c")
SWAP = [(0, 1), (1, 0)]


SCALE = 1.0 / math.sqrt(128)
LOG_SCALE = SCALE * math.log2(math.e)
MASKED = -1e30
QROWS = 512
PROWS = 256
TILE = 128


LOW, HIGH, LIVE, DIRECT, CORE, BEGIN, END = range(7)


def route(
    partner_ref, blocks_ref, segments_ref,
    table_ref, slot_ref, first_ref, far_ref, back_ref, stay_ref, arrival_ref,
):
    y, w, x = lax.axis_index("y"), lax.axis_index("w"), lax.axis_index("x")
    c = lax.axis_index("c")
    here = y * 16 + w * 4 + x
    owner = partner_ref[here]
    owner_w = (owner >> 2) & 3

    def seek(index, carry):
        far, back, stay, responder = carry
        mark = partner_ref[index]
        shift = (((mark >> 2) & 3) - w) & 3
        in_column = ((mark >> 4) == y) & ((mark & 3) == x)
        slot = ((index >> 4) << 2) | (index & 3)
        far = jnp.where(in_column & (shift == jnp.where(c == 0, 2, 1)), slot, far)
        back = jnp.where(in_column & (shift == 3), slot, back)
        stay = jnp.where(in_column & (shift == 0), slot, stay)
        return far, back, stay, jnp.where(mark == here, index, responder)

    zero = jnp.int32(0)
    far, back, stay, responder = lax.fori_loop(
        0, NY * NW * NX, seek, (zero, zero, zero, zero), unroll=8
    )
    first = zero
    for slot in range(NY * NX):
        wanted = partner_ref[(slot // NX) * 16 + w * 4 + slot % NX]
        first = first | jnp.where((((wanted >> 2) & 3) - w) & 3 < 2, 1 << slot, 0)
    segments = segments_ref[...]
    first_token = jnp.sum((segments < 1).astype(jnp.float32)).astype(jnp.int32)
    end_token = jnp.sum((segments < 2).astype(jnp.float32)).astype(jnp.int32)
    rel = (((responder >> 2) & 3) - w) & 3
    table_ref[LOW] = jnp.minimum(first_token >> 6, 7)
    table_ref[HIGH] = (end_token + 63) >> 6
    table_ref[BEGIN] = first_token
    table_ref[END] = end_token
    table_ref[LIVE] = BLK * blocks_ref[owner]
    table_ref[DIRECT] = (((owner_w - w) & 1) == c).astype(jnp.int32)
    table_ref[CORE] = c
    arrival = jnp.where((rel & 1) == c, jnp.where(rel < 2, 1, 2), 0)
    slot_ref[0] = (((owner >> 4) << 2) | (owner & 3)).astype(jnp.uint32)
    first_ref[0] = first.astype(jnp.uint32)
    far_ref[0] = far.astype(jnp.uint32)
    back_ref[0] = back.astype(jnp.uint32)
    stay_ref[0] = stay.astype(jnp.uint32)
    arrival_ref[0] = arrival.astype(jnp.uint32)


def dot(left, right, left_dim, right_dim):
    return lax.dot_general(
        left, right, (((left_dim,), (right_dim,)), ((), ())), preferred_element_type=jnp.float32
    )


def segment_marks(segments_ref):
    kinds = lax.broadcasted_iota(jnp.int32, (16, TILE), 0)
    parts = [
        jnp.where(kinds == segments_ref[pl.ds(tile, 1), :], 1.0, 0.0).astype(jnp.bfloat16)
        for tile in range(4)
    ]
    return jnp.concatenate(parts, axis=1)


def local_scores(q, keys, marks, step):
    width = TILE * (step + 1)
    shape = (QROWS, TILE)
    token = lax.broadcasted_iota(jnp.int32, shape, 0) // 4
    place = lax.broadcasted_iota(jnp.int32, shape, 1)
    owner = jnp.where(place == token, 1.0, 0.0).astype(jnp.bfloat16)
    causal = place <= token
    gate = ((1.0 - dot(owner, marks[:, width - TILE : width], 1, 1)) * MASKED).astype(jnp.bfloat16)
    scores = dot(q, keys[:width], 1, 1) + dot(gate, marks[:, :width], 1, 0)
    last = jnp.where(causal, scores[:, width - TILE :], MASKED)
    if step == 0:
        return last
    return jnp.concatenate([scores[:, : width - TILE], last], axis=1)


def local_forward(q_ref, segments_ref, kv_ref, out_ref, lse_ref):
    marks = segment_marks(segments_ref)
    for step in range(4):
        rows = pl.ds(step * QROWS, QROWS)
        width = TILE * (step + 1)
        scores = local_scores(q_ref[rows, :], kv_ref[0], marks, step)
        peak = jnp.max(scores, axis=1, keepdims=True)
        weights = jnp.exp2((scores - peak) * LOG_SCALE)
        total = jnp.sum(weights, axis=1, keepdims=True)
        mixed = dot(weights.astype(jnp.bfloat16), kv_ref[1, :width, :], 1, 0)
        out_ref[rows, :] = mixed / total
        lse_ref[rows, :] = jnp.broadcast_to(peak * LOG_SCALE + jnp.log2(total), (QROWS, TILE))


def pick(scalars_ref, got_ref, other_ref):
    return jnp.where(scalars_ref[DIRECT] == 1, got_ref[...], other_ref[...])


def prompt_step(
    scalars_ref, got_ref, other_ref, q_ref, grad_ref, outin_ref, lsein_ref,
    dprompt_ref, out_ref, lse_ref, dscore_ref,
    qbuf_ref, gradbuf_ref, outbuf_ref, lsebuf_ref, outnew_ref, lsenew_ref, dscorenew_ref,
    insems_ref, outsems_ref, dkey_ref, dvalue_ref,
):
    low_block, high_block = scalars_ref[LOW], scalars_ref[HIGH]
    coming = ((q_ref, qbuf_ref), (grad_ref, gradbuf_ref), (outin_ref, outbuf_ref), (lsein_ref, lsebuf_ref))
    leaving = ((out_ref, outnew_ref), (lse_ref, lsenew_ref), (dscore_ref, dscorenew_ref))

    def loads(index, slot):
        rows = pl.ds(pl.multiple_of(index * PROWS, PROWS), PROWS)
        return [
            pltpu.make_async_copy(far.at[rows, :], buffer.at[slot], insems_ref.at[k, slot])
            for k, (far, buffer) in enumerate(coming)
        ]

    def stores(index, slot):
        rows = pl.ds(pl.multiple_of(index * PROWS, PROWS), PROWS)
        return [
            pltpu.make_async_copy(buffer.at[slot], far.at[rows, :], outsems_ref.at[k, slot])
            for k, (far, buffer) in enumerate(leaving)
        ]

    for copy in loads(low_block, 0):
        copy.start()
    prompt = pick(scalars_ref, got_ref, other_ref)
    keys, values = prompt[:PMAX], prompt[PMAX:]
    alive = lax.broadcasted_iota(jnp.int32, (PROWS, PMAX), 1) < scalars_ref[LIVE]
    row = lax.broadcasted_iota(jnp.int32, (PROWS, PMAX), 0)
    dkey_ref[...] = jnp.zeros_like(dkey_ref)
    dvalue_ref[...] = jnp.zeros_like(dvalue_ref)

    def block(index, carry):
        slot = (index - low_block) & 1

        @pl.when(index + 1 < high_block)
        def _():
            for copy in loads(index + 1, 1 - slot):
                copy.start()

        for copy in loads(index, slot):
            copy.wait()

        @pl.when(index >= low_block + 2)
        def _():
            for copy in stores(index - 2, slot):
                copy.wait()

        first_row = index * PROWS
        q, grad = qbuf_ref[slot], gradbuf_ref[slot]
        allowed = (
            alive
            & (row >= 4 * scalars_ref[BEGIN] - first_row)
            & (row < 4 * scalars_ref[END] - first_row)
        )
        logits = jnp.where(allowed, dot(q, keys, 1, 1), MASKED) * LOG_SCALE
        lse = lsebuf_ref[slot][:, :1]
        peak = jnp.maximum(lse, jnp.max(logits, axis=1, keepdims=True))
        weights = jnp.exp2(logits - peak)
        before = jnp.exp2(lse - peak)
        total = before + jnp.sum(weights, axis=1, keepdims=True)
        inverse = 1.0 / total
        probabilities = weights * inverse
        low = probabilities.astype(jnp.bfloat16)
        out = outbuf_ref[slot] * (before * inverse) + dot(low, values, 1, 0)
        outnew_ref[slot] = out
        lsenew_ref[slot] = jnp.broadcast_to(peak + jnp.log2(total), (PROWS, TILE))
        rounded = out.astype(jnp.bfloat16).astype(jnp.float32)
        delta = jnp.sum(grad.astype(jnp.float32) * rounded, axis=1, keepdims=True)
        dscore = (probabilities * (dot(grad, values, 1, 1) - delta)).astype(jnp.bfloat16)
        dscorenew_ref[slot, :, :PMAX] = dscore
        for copy in stores(index, slot):
            copy.start()
        dvalue_ref[...] += dot(low, grad, 0, 0)
        dkey_ref[...] += dot(dscore, q, 0, 0)
        return carry

    lax.fori_loop(low_block, high_block, block, 0)
    dprompt_ref[:PMAX, :] = (dkey_ref[...] * SCALE).astype(jnp.bfloat16)
    dprompt_ref[PMAX:, :] = dvalue_ref[...].astype(jnp.bfloat16)
    for back in (2, 1):
        @pl.when(high_block - back >= low_block)
        def _():
            for copy in stores(high_block - back, (high_block - back - low_block) & 1):
                copy.wait()


def local_backward(
    scalars_ref, q_ref, grad_ref, segments_ref, kv_ref, got_ref, other_ref,
    outlocal_ref, lselocal_ref, outprompt_ref, lseprompt_ref, dscore_ref,
    attention_ref, dquery_ref, kept_ref, given_ref, dkey_ref, dvalue_ref, acc_ref,
):
    def chosen(prompt_ref, local_ref, step):
        parts = []
        for part in range(QROWS // PROWS):
            index = step * (QROWS // PROWS) + part
            inside = (scalars_ref[LOW] <= index) & (index < scalars_ref[HIGH])
            rows = pl.ds(index * PROWS, PROWS)
            parts.append(jnp.where(inside, prompt_ref[rows, :], local_ref[rows, :]))
        return jnp.concatenate(parts, axis=0)

    dkey_ref[...] = jnp.zeros_like(dkey_ref)
    dvalue_ref[...] = jnp.zeros_like(dvalue_ref)
    prompt_keys = pick(scalars_ref, got_ref, other_ref)[:PMAX]
    marks = segment_marks(segments_ref)
    for step in range(4):
        rows = pl.ds(step * QROWS, QROWS)
        width = TILE * (step + 1)
        q, grad = q_ref[rows, :], grad_ref[rows, :]
        attention = chosen(outprompt_ref, outlocal_ref, step).astype(jnp.bfloat16)
        attention_ref[rows, :] = attention
        delta = jnp.sum(
            grad.astype(jnp.float32) * attention.astype(jnp.float32), axis=1, keepdims=True
        )
        scores = local_scores(q, kv_ref[0], marks, step)
        lse = chosen(lseprompt_ref, lselocal_ref, step)
        if step:
            lse = jnp.concatenate([lse] * (step + 1), axis=1)
        probabilities = jnp.exp2(scores * LOG_SCALE - lse)
        low = probabilities.astype(jnp.bfloat16)
        dprob = dot(grad, kv_ref[1, :width, :], 1, 1)
        dscore = (probabilities * (dprob - delta)).astype(jnp.bfloat16)
        acc_ref[...] = dot(dscore, kv_ref[0, :width, :], 1, 0)
        dvalue_ref[:width, :] += dot(low, grad, 0, 0)
        dkey_ref[:width, :] += dot(dscore, q, 0, 0)
        for part in range(QROWS // PROWS):
            index = step * (QROWS // PROWS) + part

            @pl.when((scalars_ref[LOW] <= index) & (index < scalars_ref[HIGH]))
            def _():
                acc_ref[pl.ds(part * PROWS, PROWS), :] += dot(
                    dscore_ref[pl.ds(index * PROWS, PROWS), :PMAX], prompt_keys, 1, 0
                )

        dquery_ref[rows, :] = (acc_ref[...] * SCALE).astype(jnp.bfloat16)
    dkey = dkey_ref[...] * SCALE
    dvalue = dvalue_ref[...]
    keep_key = scalars_ref[CORE] == 0
    kept_ref[...] = jnp.where(keep_key, dkey, dvalue).astype(jnp.bfloat16)
    given_ref[...] = jnp.where(keep_key, dvalue, dkey).astype(jnp.bfloat16)


SMEM = pl.BlockSpec(memory_space=pltpu.SMEM)
VMEM = pl.BlockSpec(memory_space=pltpu.VMEM)
FAR = pl.BlockSpec(memory_space=pltpu.HBM)


def near(array):
    return pltpu.with_memory_space_constraint(array, pltpu.VMEM)


def body(queries, keys_values, grad_out, segments, partner, prompt_blocks):
    rows_here = queries.shape[0]
    heads_here = queries.shape[1]
    head_dim = queries.shape[2]
    flat = rows_here * heads_here
    y, w, x = lax.axis_index("y"), lax.axis_index("w"), lax.axis_index("x")
    h, c = lax.axis_index("h"), lax.axis_index("c")

    zero = jnp.uint32(0)

    def prompt_of(head):
        rows = lax.dynamic_slice(
            keys_values, (zero, zero, head.astype(jnp.uint32), zero), (PMAX, 2, 1, head_dim)
        )
        return jnp.transpose(rows[:, :, 0], (1, 0, 2)).reshape(2 * PMAX, head_dim)

    far_sender = (h < 2) | (h >= 6)
    head_far = jnp.where(h < 2, 2 * h + c + 4, 2 * h + c - 12)
    head_next = 2 * h + 1 - c - 4
    far_or_next = lax.ppermute(
        prompt_of(jnp.where(far_sender, head_far, head_next)), RUN,
        run_pairs(FORWARD_FAR + FORWARD_NEXT),
    )
    back = lax.ppermute(
        prompt_of((2 * h + c) & (NH - 1)), RUN, run_pairs(FORWARD_BACK)
    )
    own = prompt_of(h)

    one = jax.ShapeDtypeStruct((1,), jnp.uint32)
    table, *scalar = pl.pallas_call(
        route, out_shape=(jax.ShapeDtypeStruct((16,), jnp.int32),) + (one,) * 6, name="route",
        in_specs=[SMEM, SMEM, VMEM], out_specs=(SMEM,) * 7,
    )(partner, prompt_blocks, segments.reshape(-1, TILE))
    to_slot, first_bits, far_slot, back_slot, stay_slot, arrival = (s.reshape(()) for s in scalar)

    kv_mixed = lax.dynamic_index_in_dim(keys_values, h.astype(jnp.uint32), 2, keepdims=False)
    tiles = segments.reshape(-1, TILE)
    q = queries.reshape(flat, head_dim)
    grad = grad_out.reshape(flat, head_dim)

    wide = pltpu.HBM((flat, head_dim), jnp.float32)
    narrow = jax.ShapeDtypeStruct((flat, head_dim), jnp.bfloat16)
    part_shape = jax.ShapeDtypeStruct((rows_here, head_dim), jnp.bfloat16)

    slots = jnp.arange(NY * NX, dtype=jnp.uint32)
    first = jnp.where(c == 0, own, back)
    take_first = (first_bits >> slots) & 1 == 1
    outgoing = jnp.where(take_first[:, None, None], first[None], far_or_next[None])
    outgoing, kv_mixed = lax.optimization_barrier((outgoing, kv_mixed))
    kv_local = jnp.transpose(kv_mixed, (1, 0, 2))
    incoming = lax.all_to_all(outgoing, ("y", "x"), split_axis=0, concat_axis=0, tiled=True)
    local_out, local_lse = pl.pallas_call(
        local_forward, out_shape=(wide, wide), name="local_forward",
        in_specs=[VMEM] * 3, out_specs=(VMEM, VMEM),
    )(q, tiles, kv_local)
    incoming, local_out, local_lse = lax.optimization_barrier((incoming, local_out, local_lse))
    got = lax.dynamic_index_in_dim(incoming, to_slot, 0, keepdims=False)
    other = lax.ppermute(got, "c", SWAP)

    dprompt, out, lse, dscore = pl.pallas_call(
        prompt_step,
        out_shape=(
            pltpu.VMEM((2 * PMAX, head_dim), jnp.bfloat16), wide, wide,
            pltpu.HBM((flat, TILE), jnp.bfloat16),
        ),
        in_specs=[SMEM, VMEM, VMEM] + [FAR] * 4,
        out_specs=(VMEM, FAR, FAR, FAR),
        scratch_shapes=(
            [pltpu.VMEM((2, PROWS, head_dim), jnp.bfloat16)] * 2
            + [pltpu.VMEM((2, PROWS, head_dim), jnp.float32)] * 4
            + [pltpu.VMEM((2, PROWS, TILE), jnp.bfloat16)]
            + [pltpu.SemaphoreType.DMA((4, 2)), pltpu.SemaphoreType.DMA((3, 2))]
            + [pltpu.VMEM((PMAX, head_dim), jnp.float32)] * 2
        ),
        name="prompt_step",
    )(table, near(got), near(other), q, grad, local_out, local_lse)

    total = dprompt.astype(jnp.float32) + lax.ppermute(dprompt, "c", SWAP).astype(jnp.float32)
    spread = jnp.where(
        (slots < NY * NX + y.astype(jnp.uint32))[:, None, None], total.astype(jnp.bfloat16)[None],
        jnp.zeros((), jnp.bfloat16),
    )
    spread = lax.all_to_all(spread, ("y", "x"), split_axis=0, concat_axis=0, tiled=True)

    def parcel(slot):
        return lax.dynamic_index_in_dim(spread, slot, 0, keepdims=False)

    far_or_next_back = lax.ppermute(
        parcel(far_slot), RUN, run_pairs(BACKWARD_FAR + BACKWARD_NEXT)
    )
    back_back = lax.ppermute(parcel(back_slot), RUN, run_pairs(BACKWARD_BACK))
    stay = parcel(stay_slot)

    attention, query_gradient, kept, given = pl.pallas_call(
        local_backward,
        out_shape=(narrow, narrow, part_shape, part_shape),
        name="local_backward",
        in_specs=[SMEM] + [VMEM] * 11,
        out_specs=(VMEM,) * 4,
        scratch_shapes=[pltpu.VMEM((rows_here, head_dim), jnp.float32)] * 3,
    )(
        table, q, grad, tiles, kv_local, got, other,
        local_out, local_lse, out, lse, dscore,
    )
    swapped = lax.ppermute(given, "c", SWAP)
    own_sum = kept.astype(jnp.float32) + swapped.astype(jnp.float32)

    arrived = jnp.where(c == 0, stay, back_back)
    arrived = jnp.where(arrival == 2, far_or_next_back, arrived)
    arrived = jnp.where(arrival == 0, jnp.zeros((), arrived.dtype), arrived)
    keep_row = (c * PMAX).astype(jnp.uint32)
    kept_prompt = lax.dynamic_slice(arrived, (keep_row, zero), (PMAX, head_dim))
    given_prompt = lax.dynamic_slice(arrived, (PMAX - keep_row, zero), (PMAX, head_dim))
    swapped_prompt = lax.ppermute(given_prompt, "c", SWAP)
    prompt_rows = (
        own_sum[:PMAX] + kept_prompt.astype(jnp.float32) + swapped_prompt.astype(jnp.float32)
    )
    kv_result = lax.dynamic_update_slice(
        own_sum.astype(jnp.bfloat16), prompt_rows.astype(jnp.bfloat16), (0, 0)
    )
    return (
        attention.reshape(queries.shape), query_gradient.reshape(queries.shape), kv_result
    )


def solution(mesh):
    fine = Mesh(mesh.devices.reshape(NY, NW, NX, NH, NC), ("y", "w", "x", "h", "c"))
    seq, head = ("y", "w", "x"), ("h", "c")
    in_specs = (
        P(seq, head, None),
        P(seq, None, None, None),
        P(seq, head, None),
        P(seq),
        P(),
        P(),
    )
    out_specs = (P(seq, head, None), P(seq, head, None), P(seq, head))
    return jax.shard_map(body, mesh=fine, in_specs=in_specs, out_specs=out_specs, check_vma=False)
```
